256 devices in a mesh: ctx: 32 (over y, z), tp: 8 (over x, core).
Axes of the slice: x: 4, y: 4, z: 8, core: 2. Of those that a mesh axis runs over, the one named last changes fastest.
Arguments:
- prompt_states: bfloat16 [16384, 5376], P('ctx', 'tp'), may hold values from -400 to 400
- decode_states: bfloat16 [512, 5376], P('ctx', 'tp'), may hold values from -400 to 400
- norm_gain: float32 [5376], replicated, may hold values from 0.25 to 1.75
- query_weight: bfloat16 [5376, 4096], P(None, 'tp'), may hold values from -0.078125 to 0.078125
- key_weight: bfloat16 [5376, 2048], P(None, 'tp'), may hold values from -0.078125 to 0.078125
- value_weight: bfloat16 [5376, 2048], P(None, 'tp'), may hold values from -0.078125 to 0.078125
- query_gain: float32 [128], replicated, may hold values from 1 to 20
- key_gain: float32 [128], replicated, may hold values from 1 to 20
- prompt_lengths: int32 [4], replicated, may hold values from 2049 to 4096, as said below
- row_prompt: int32 [512], P('ctx'), may hold values from 0 to 3
Outputs:
- prefill_attention: bfloat16 [16384, 4096], P('ctx', 'tp')
- decode_attention: bfloat16 [512, 4096], P('ctx', 'tp')
The draws below stay inside these ranges and needn't reach their ends.
Inputs may be any that keep to these rules, and one draw needn't show every extreme that they name: `prompt_lengths`: every prompt has more than half of its 4096 slots live and one prompt fills all of them.
All inputs are finite; a program needn't handle non-finite values.
Results may differ from the reference program's by a relative error of at most 0.02.
The reference program's roundings to bfloat16 on the way count: a program that leaves them out, or rounds other values in their place, can miss the bound.
Values may be sent and summed in bfloat16 or wider, within the bound.
A program may use at most 128 MiB of HBM per device.

```python
import math
import jax
import jax.numpy as jnp
from jax import lax

D = 5376
QH = 32
KVH = 16
HD = 128
WINDOW = 1024
PROMPTS = 4
TOK_DEV = 512
DEC_DEV = 16
TOKENS = 16384
SLOT = 4096
DEC_ROWS = 512
N_CTX = 32


def scaled_states(key, row_count, salt):
    row_scale = jnp.exp(jax.random.uniform(jax.random.fold_in(key, salt + 2), (row_count, 1), minval=0.0, maxval=math.log(10.0)))
    column_scale = jnp.exp(jax.random.uniform(jax.random.fold_in(key, 300), (1, D), minval=0.0, maxval=math.log(10.0)))
    base_values = jnp.clip(jax.random.normal(jax.random.fold_in(key, salt + 1), (row_count, D)), -4.0, 4.0)
    values = base_values * row_scale * column_scale
    return values.astype(jnp.bfloat16)


def draw_prompt_states(key, part):
    return scaled_states(key, TOKENS, 100)


def draw_decode_states(key, part):
    return scaled_states(key, DEC_ROWS, 200)


def head_gain(key, salt):
    values = jnp.exp(jax.random.uniform(jax.random.fold_in(key, salt), (HD,), minval=0.0, maxval=math.log(3.0)))
    return values.astype(jnp.float32)


def draw_query_gain(key, part):
    return head_gain(key, 600)


def draw_key_gain(key, part):
    return head_gain(key, 700)


def draw_prompt_lengths(key, part):
    base_values = jax.random.randint(jax.random.fold_in(key, 11), (PROMPTS,), SLOT // 2 + 1, SLOT + 1)
    full_prompt = jax.random.randint(jax.random.fold_in(key, 12), (), 0, PROMPTS)
    return jnp.where(jnp.arange(PROMPTS) == full_prompt, SLOT, base_values).astype(jnp.int32)


def plant(array, own_key, least, high):
    index_at = [jax.random.randint(jax.random.fold_in(own_key, axis), (), 0, length) for axis, length in enumerate(array.shape)]
    longest = array.shape.index(max(array.shape))
    next_to = index_at[:longest] + [(index_at[longest] + 1) % array.shape[longest]] + index_at[longest + 1:]
    return array.at[tuple(index_at)].set(least).at[tuple(next_to)].set(high)


def level_of(key, shape, cuts, low, top_value):
    def one(dim, parts):
        heights = jax.random.uniform(jax.random.fold_in(jax.random.fold_in(key, 6), dim), (parts,), jnp.float32, low / len(cuts), top_value / len(cuts))
        return jnp.repeat(jnp.exp(heights), shape[dim] // parts).reshape((-1,) + (1,) * (len(shape) - dim - 1))

    factor_of = one(*cuts[0])
    for cut in cuts[1:]:
        factor_of = factor_of * one(*cut)
    return factor_of


def centred(key, dims, width, reach, split=(), kind=jnp.bfloat16):
    gain = level_of(key, dims, split, -0.22, 0.18) if split else 1.0
    entries = jax.random.normal(key, dims, jnp.float32) * width * gain
    return jnp.minimum(jnp.maximum(entries, -reach), reach).astype(kind)


def setup_inputs(seed: int = 0) -> dict:
    key_of = jax.random.split(jax.random.key(seed), 11)
    return {
        "prompt_states": draw_prompt_states(jax.random.fold_in(key_of[10], 71), 0),
        "decode_states": draw_decode_states(jax.random.fold_in(key_of[10], 71), 0),
        "norm_gain": jnp.clip(1.0 + 0.15 * jax.random.normal(key_of[2], (D,), jnp.float32), 0.25, 1.75),
        "query_weight": centred(key_of[3], (D, QH * HD), D ** -0.5, 0.078125, ((1, 8),)),
        "key_weight": centred(key_of[4], (D, KVH * HD), D ** -0.5, 0.078125, ((1, 8),)),
        "value_weight": centred(key_of[5], (D, KVH * HD), D ** -0.5, 0.078125, ((1, 8),)),
        "query_gain": draw_query_gain(jax.random.fold_in(key_of[10], 71), 0),
        "key_gain": draw_key_gain(jax.random.fold_in(key_of[10], 71), 0),
        "prompt_lengths": draw_prompt_lengths(jax.random.fold_in(key_of[10], 71), 0),
        "row_prompt": plant(jax.random.randint(key_of[9], (DEC_ROWS,), 0, PROMPTS), jax.random.fold_in(key_of[9], 1), 0, PROMPTS - 1).astype(jnp.int32),
    }


EPS = 1e-06
SCORE_SCALE = 168.0 ** (-0.5)

def rotate(vectors, positions):
    half_size = vectors.shape[-1] // 2
    frequency = 10000.0 ** (-(jnp.arange(half_size, dtype=jnp.float32) * 2.0) / vectors.shape[-1])
    angles = positions.astype(jnp.float32)[:, None, None] * frequency
    cosine = jnp.cos(angles)
    sine_part = jnp.sin(angles)
    first_half = vectors[..., :half_size]
    second_half = vectors[..., half_size:]
    return jnp.concatenate([first_half * cosine - second_half * sine_part, second_half * cosine + first_half * sine_part], axis=-1)

def head_norm(vectors, gain_values):
    return vectors * lax.rsqrt(lax.optimization_barrier(jnp.mean(vectors * vectors, axis=-1, keepdims=True)) + EPS) * gain_values

def project(states, positions, norm_gain, query_weight, key_weight, value_weight, query_gain, key_gain):
    widened = states.astype(jnp.float32)
    scaled = (widened * norm_gain).astype(jnp.bfloat16)
    inverse = lax.rsqrt(lax.optimization_barrier(jnp.mean(widened * widened, axis=1)) + EPS)[:, None]
    row_count = states.shape[0]
    head_size = query_gain.shape[0]
    query_heads = jnp.dot(scaled, query_weight, preferred_element_type=jnp.float32) * inverse
    key_heads = jnp.dot(scaled, key_weight, preferred_element_type=jnp.float32) * inverse
    value_heads = jnp.dot(scaled, value_weight, preferred_element_type=jnp.float32) * inverse
    query_heads = rotate(head_norm(query_heads.reshape(row_count, -1, head_size), query_gain), positions).astype(jnp.bfloat16)
    key_heads = rotate(head_norm(key_heads.reshape(row_count, -1, head_size), key_gain), positions).astype(jnp.bfloat16)
    value_heads = value_heads.reshape(row_count, -1, head_size).astype(jnp.bfloat16)
    return (query_heads, key_heads, value_heads)

def window_mask(query_index, key_index, slot_size):
    later = key_index[None, :]
    earlier = query_index[:, None]
    return (later >= 0) & (later // slot_size == earlier // slot_size) & (later <= earlier) & (later > earlier - WINDOW)

def prompt_order(values):
    blocks_per = N_CTX // PROMPTS
    shaped = values.reshape((blocks_per, PROMPTS) + values.shape[1:])
    order = (1, 0) + tuple(range(2, shaped.ndim))
    return jnp.transpose(shaped, order).reshape((TOKENS,) + values.shape[2:])

def reference(prompt_states, decode_states, norm_gain, query_weight, key_weight, value_weight, query_gain, key_gain, prompt_lengths, row_prompt):
    group_size = QH // KVH
    block_positions = ((jnp.arange(N_CTX, dtype=jnp.int32) // PROMPTS)[:, None] * TOK_DEV + jnp.arange(TOK_DEV, dtype=jnp.int32)[None, :]).astype(jnp.int32)

    def project_block(block_pair):
        return project(block_pair[0], block_pair[1], norm_gain, query_weight, key_weight, value_weight, query_gain, key_gain)
    query_blocks, key_blocks, value_blocks = lax.map(project_block, (prompt_states.reshape(N_CTX, TOK_DEV, D), block_positions))
    query_heads = prompt_order(query_blocks)
    key_heads = prompt_order(key_blocks)
    value_heads = prompt_order(value_blocks)
    token_index = jnp.arange(TOKENS, dtype=jnp.int32)
    front_rows = jnp.zeros((WINDOW, KVH, HD), jnp.bfloat16)
    padded_keys = jnp.concatenate([front_rows, key_heads], axis=0)
    padded_values = jnp.concatenate([front_rows, value_heads], axis=0)
    row_lengths = prompt_lengths[token_index // SLOT]

    def attend_block(block_index):
        block_start = (block_index * TOK_DEV).astype(jnp.int32)
        block_query = lax.dynamic_slice_in_dim(query_heads, block_start, TOK_DEV, 0).reshape(TOK_DEV, KVH, group_size, HD)
        block_keys = lax.dynamic_slice_in_dim(padded_keys, block_start, WINDOW + TOK_DEV, 0)
        block_values = lax.dynamic_slice_in_dim(padded_values, block_start, WINDOW + TOK_DEV, 0)
        query_index = block_start + jnp.arange(TOK_DEV, dtype=jnp.int32)
        key_index = block_start - WINDOW + jnp.arange(WINDOW + TOK_DEV, dtype=jnp.int32)
        scores = jnp.einsum('tkgd,skd->kgts', block_query.astype(jnp.float32), block_keys.astype(jnp.float32), precision=lax.Precision.HIGHEST) * SCORE_SCALE
        visible = window_mask(query_index, key_index, SLOT)
        row_top = lax.optimization_barrier(jnp.max(jnp.where(visible, scores, -jnp.inf), axis=-1, keepdims=True))
        weights = jnp.where(visible, jnp.exp(scores - row_top), 0.0)
        weight_sum = lax.optimization_barrier(jnp.sum(weights, axis=-1))
        short_weights = lax.optimization_barrier(weights.astype(jnp.bfloat16))
        mixture = jnp.einsum('kgts,skd->tkgd', short_weights.astype(jnp.float32), block_values.astype(jnp.float32), precision=lax.Precision.HIGHEST)
        mixture = mixture / jnp.transpose(weight_sum, (2, 0, 1))[..., None]
        alive_rows = query_index % SLOT < lax.dynamic_slice_in_dim(row_lengths, block_start, TOK_DEV, 0)
        return jnp.where(alive_rows[:, None, None, None], mixture, 0.0).astype(jnp.bfloat16).reshape(TOK_DEV, QH * HD)
    ordered = lax.map(attend_block, jnp.arange(N_CTX, dtype=jnp.int32)).reshape(PROMPTS, N_CTX // PROMPTS, TOK_DEV, QH * HD)
    prefill_attention = jnp.transpose(ordered, (1, 0, 2, 3)).reshape(TOKENS, QH * HD)
    tail_start = (jnp.arange(PROMPTS, dtype=jnp.int32) * SLOT + prompt_lengths - WINDOW).astype(jnp.int32)
    tail_keys = jax.vmap(lambda start_row: lax.dynamic_slice_in_dim(key_heads, start_row, WINDOW, 0))(tail_start)
    tail_values = jax.vmap(lambda start_row: lax.dynamic_slice_in_dim(value_heads, start_row, WINDOW, 0))(tail_start)
    decode_positions = prompt_lengths[row_prompt]
    decode_query, decode_keys, decode_values = project(decode_states, decode_positions, norm_gain, query_weight, key_weight, value_weight, query_gain, key_gain)

    def decode_block(block_index):
        block_start = (block_index * DEC_DEV).astype(jnp.int32)
        chosen = lax.dynamic_slice_in_dim(row_prompt, block_start, DEC_DEV, 0)
        block_query = lax.dynamic_slice_in_dim(decode_query, block_start, DEC_DEV, 0).reshape(DEC_DEV, KVH, group_size, HD)
        own_keys = lax.dynamic_slice_in_dim(decode_keys, block_start, DEC_DEV, 0)
        own_values = lax.dynamic_slice_in_dim(decode_values, block_start, DEC_DEV, 0)
        cache_keys = jnp.concatenate([tail_keys[chosen], own_keys[:, None]], axis=1)
        cache_values = jnp.concatenate([tail_values[chosen], own_values[:, None]], axis=1)
        scores = jnp.einsum('rkgd,rskd->rkgs', block_query.astype(jnp.float32), cache_keys.astype(jnp.float32), precision=lax.Precision.HIGHEST) * SCORE_SCALE
        row_top = lax.optimization_barrier(jnp.max(scores, axis=-1, keepdims=True))
        weights = jnp.exp(scores - row_top)
        weight_sum = lax.optimization_barrier(jnp.sum(weights, axis=-1))
        short_weights = lax.optimization_barrier(weights.astype(jnp.bfloat16))
        mixture = jnp.einsum('rkgs,rskd->rkgd', short_weights.astype(jnp.float32), cache_values.astype(jnp.float32), precision=lax.Precision.HIGHEST)
        mixture = mixture / weight_sum[..., None]
        return mixture.astype(jnp.bfloat16).reshape(DEC_DEV, QH * HD)
    decode_attention = lax.map(decode_block, jnp.arange(N_CTX, dtype=jnp.int32)).reshape(DEC_ROWS, QH * HD)
    return (prefill_attention, decode_attention)
```

```python
import functools
import math

import jax
import jax.numpy as jnp
import numpy as np
from jax import lax
from jax.experimental import pallas as pl
from jax.experimental.pallas import tpu as pltpu
from jax.sharding import PartitionSpec as P

MESH = pl.DeviceIdType.MESH
F32, BF16 = jnp.float32, jnp.bfloat16
WINDOW = 1024
PROMPTS = 4
EPS = 1e-06
SCORE_SCALE = 168.0 ** (-0.5)
HD = 128
NY, NZ, NX = 4, 8, 4
CH = 128
NCH = 4
NEG = -1e30


def dot(a, b, dims):
    return lax.dot_general(a, b, (dims, ((), ())), preferred_element_type=F32)


def kernel(
    feature_count,
    x_ref, xd_ref, gcol_ref, grow_ref, rp_ref, freq_ref, sgn_ref, qg_ref, kg_ref, len_ref,
    wq_hbm, wk_hbm, wv_hbm,
    out_ref, dout_ref,
    xg, xd, ss, wkv, wq, kv, relay, q_s, dqg, dk_s, dv_s, dpart, b1, p2, b2,
    ag_send, ag_recv, wsem, h_send, h_recv,
    dq1_send, dq1_recv, dq2_send, dq2_recv, r1_send, r1_recv, r2_send, r2_recv,
):
    me_c = lax.axis_index("ctx")
    me_t = lax.axis_index("tp")
    x, c = me_t // 2, lax.rem(me_t, 2)
    y, z = me_c // NZ, lax.rem(me_c, NZ)
    way = 1 - 2 * c
    feat = x_ref.shape[0]
    block = 2 * y + z // 4
    prompt = lax.rem(z, PROMPTS)

    def tp_of(xx, cc):
        return lax.rem(xx + NX, NX) * 2 + cc

    def ctx_of(yy, zz):
        return lax.rem(yy + NY, NY) * NZ + lax.rem(zz + NZ, NZ)

    near_a, near_b, far = tp_of(x - way, c), tp_of(x + way, c), tp_of(x + 2, c)
    partner = tp_of(x, 1 - c)
    from_partner = (partner, tp_of(x + way, 1 - c), tp_of(x - way, 1 - c), tp_of(x + 2, 1 - c))
    z_two, z_two_in = z + 2 * way, z - 2 * way
    source_z = lax.rem(z_two_in + NZ, NZ)
    out_b1 = ctx_of(y + source_z // 4, z_two)
    in_b1 = ctx_of(y - (1 - z // 4), z_two_in)

    weights = (
        pltpu.make_async_copy(wk_hbm, wkv.at[:, 0:256], wsem.at[0]),
        pltpu.make_async_copy(wv_hbm, wkv.at[:, 256:512], wsem.at[1]),
        pltpu.make_async_copy(wq_hbm, wq, wsem.at[2]),
    )
    for copy in weights:
        copy.start()

    barrier = pltpu.get_barrier_semaphore()
    for device in (
        [(me_c, t) for t in (near_a, near_b, partner)]
        + [(ctx_of(y, z + j), me_t) for j in range(1, NZ)]
        + [(ctx_of(y + j, z), me_t) for j in range(1, NY)]
        + [(in_b1, me_t)]
    ):
        pl.semaphore_signal(barrier, inc=1, device_id=device, device_id_type=MESH)

    decode_wide = xd_ref[...].astype(F32)
    xd[me_t] = (decode_wide * grow_ref[...]).astype(BF16)
    decode_sum = jnp.sum(decode_wide * decode_wide, axis=1, keepdims=True)
    ss[me_t, 4:6] = jnp.broadcast_to(decode_sum, (16, 128)).reshape(2, 8, 128)
    for k in range(NCH):
        wide = x_ref[:, k * CH : (k + 1) * CH].astype(F32)
        xg[k, me_t] = (wide * gcol_ref[...]).astype(BF16)
        ss[me_t, k] = jnp.sum((wide * wide).reshape(feat // 8, 8, CH), axis=0)

    pl.semaphore_wait(barrier, 14)

    def piece(k, d):
        if isinstance(k, int) and k == 4:
            return xd.at[d]
        if isinstance(k, int) and k == 5:
            return ss.at[d]
        return xg.at[k, d]

    def ag(k, d, j, target):
        return pltpu.make_async_remote_copy(
            src_ref=piece(k, d), dst_ref=piece(k, d),
            send_sem=ag_send.at[k, j], recv_sem=ag_recv.at[k, j],
            device_id=(me_c, target), device_id_type=MESH,
        )

    def start_own(k):
        ag(k, me_t, 0, near_b).start()
        ag(k, me_t, 1, near_a).start()
        ag(k, me_t, 3, partner).start()

    def phase_a(k):
        ag(k, near_a, 0, near_b).wait_recv()
        ag(k, near_a, 2, near_b).start()
        ag(k, near_a, 4, partner).start()

    def phase_b(k):
        ag(k, near_b, 1, near_b).wait_recv()
        ag(k, near_b, 5, partner).start()

    def phase_c(k):
        ag(k, far, 2, near_b).wait_recv()
        ag(k, far, 6, partner).start()
        for j in range(4):
            ag(k, from_partner[j], 3 + j, near_b).wait_recv()

    def ag_sent(k):
        for j in range(7):
            ag(k, me_t, j, near_b).wait_send()

    def halo(kind, s):
        src, dst, target = (
            (kv.at[8 + s], kv.at[s], ctx_of(y + 1, z)),
            (kv.at[8 + s], relay.at[s], ctx_of(y, z_two)),
            (relay.at[s], kv.at[4 + s], out_b1),
        )[kind]
        return pltpu.make_async_remote_copy(
            src_ref=src, dst_ref=dst, send_sem=h_send.at[kind, s], recv_sem=h_recv.at[kind, s],
            device_id=(target, me_t), device_id_type=MESH,
        )

    def pass_on(s):
        halo(1, s).wait_recv()
        halo(2, s).start()

    freq, sgn = freq_ref[...], sgn_ref[...]

    def rope_tables(positions):
        angles = positions * freq
        return jnp.cos(angles), jnp.sin(angles) * sgn

    def head(acc, gain, tables):
        unit = acc * lax.rsqrt(jnp.mean(acc * acc, axis=1, keepdims=True) + EPS) * gain
        return (unit * tables[0] + pltpu.roll(unit, HD // 2, axis=1) * tables[1]).astype(BF16)

    qg, kg = qg_ref[...], kg_ref[...]

    start_own(5)
    start_own(4)
    start_own(0)
    start_own(1)
    for k in (5, 4):
        phase_a(k)
        phase_b(k)
    for k in (5, 4):
        phase_c(k)

    for copy in weights:
        copy.wait()
    acc_kv = jnp.zeros((16, 512), F32)
    acc_q = jnp.zeros((16, 512), F32)
    for d in range(8):
        rows = slice(d * feat, (d + 1) * feat)
        acc_kv += dot(xd[d], wkv[rows, :], ((1,), (0,)))
        acc_q += dot(xd[d], wq[rows, :], ((1,), (0,)))
    rp = rp_ref[...]
    decode_pos = jnp.zeros((16, 128), jnp.int32)
    for p in range(PROMPTS):
        decode_pos = jnp.where(rp == p, len_ref[p], decode_pos)
    tables = rope_tables(decode_pos.astype(F32))
    sums = jnp.sum(ss[:, 4:6], axis=0).reshape(16, 128)
    inverse = lax.rsqrt(sums / feature_count + EPS)
    for h in range(4):
        dqg[me_c, :, h * HD : (h + 1) * HD] = head(
            acc_q[:, h * HD : (h + 1) * HD] * inverse, qg, tables
        )
    for h in range(2):
        dk_s[:, h * HD : (h + 1) * HD] = head(
            acc_kv[:, h * HD : (h + 1) * HD] * inverse, kg, tables
        )
        dv_s[:, h * HD : (h + 1) * HD] = (
            acc_kv[:, 256 + h * HD : 256 + (h + 1) * HD] * inverse
        ).astype(BF16)

    def dq1(j, owner_z, target_z):
        slot = dqg.at[ctx_of(y, owner_z)]
        return pltpu.make_async_remote_copy(
            src_ref=slot, dst_ref=slot, send_sem=dq1_send.at[j - 1], recv_sem=dq1_recv.at[j - 1],
            device_id=(ctx_of(y, target_z), me_t), device_id_type=MESH,
        )

    def dq2(j, owner_y, target_y):
        slots = dqg.at[pl.ds(lax.rem(owner_y + NY, NY) * NZ, NZ)]
        return pltpu.make_async_remote_copy(
            src_ref=slots, dst_ref=slots, send_sem=dq2_send.at[j - 1], recv_sem=dq2_recv.at[j - 1],
            device_id=(ctx_of(target_y, z), me_t), device_id_type=MESH,
        )

    for j in range(1, NZ):
        dq1(j, z, z + j).start()

    row_index = lax.broadcasted_iota(jnp.int32, (CH, 1), 0)
    phase_a(0)
    start_own(2)
    phase_b(0)

    def project(s, carry):
        @pl.when(s < NCH - 1)
        def _():
            phase_a(s + 1)

        @pl.when(s < NCH - 3)
        def _():
            start_own(s + 3)

        @pl.when(s < NCH - 1)
        def _():
            phase_b(s + 1)

        phase_c(s)
        states = xg[s].reshape(8 * feat, CH)
        sums = jnp.sum(jnp.transpose(jnp.sum(ss[:, s], axis=0)), axis=1, keepdims=True)
        inverse = lax.rsqrt(sums / feature_count + EPS)
        tables = rope_tables((block * 512 + s * CH + row_index).astype(F32))
        acc = dot(states, wkv[...], ((0,), (0,)))
        for h in range(2):
            kv[8 + s, :, h * HD : (h + 1) * HD] = head(
                acc[:, h * HD : (h + 1) * HD] * inverse, kg, tables
            )
        kv[8 + s, :, 256:512] = (acc[:, 256:512] * inverse).astype(BF16)
        halo(0, s).start()
        halo(1, s).start()
        acc = dot(states, wq[...], ((0,), (0,)))
        for h in range(4):
            q_s[s, :, h * HD : (h + 1) * HD] = head(
                acc[:, h * HD : (h + 1) * HD] * inverse, qg, tables
            )

        @pl.when(s > 0)
        def _():
            pass_on(s - 1)

        @pl.when(s == 0)
        def _():
            for j in range(1, NZ):
                dq1(j, z - j, z).wait_recv()
            for j in range(1, NY):
                dq2(j, y, y + j).start()

        return carry

    lax.fori_loop(0, NCH, project, 0)
    pass_on(NCH - 1)

    for j in range(1, NY):
        dq2(j, y - j, y).wait_recv()
    length = len_ref[prompt]
    key_pos = block * 512 + lax.broadcasted_iota(jnp.int32, (1, 512), 1)
    bias = jnp.where((key_pos >= length - WINDOW) & (key_pos < length), 0.0, NEG)
    lane = lax.broadcasted_iota(jnp.int32, (1, 128), 1)

    def pack(lse_list):
        packed = None
        for h, lse in enumerate(lse_list):
            high = lse.astype(BF16).astype(F32)
            middle = (lse - high).astype(BF16).astype(F32)
            low = lse - high - middle
            term = (
                jnp.where(lane == h, high, 0.0)
                + jnp.where(lane == 4 + h, middle, 0.0)
                + jnp.where(lane == 8 + h, low, 0.0)
            )
            packed = term if packed is None else packed + term
        return packed.astype(BF16)

    def lse_of(packed, h):
        wide = packed.astype(F32)
        return wide[:, h : h + 1] + wide[:, 4 + h : 5 + h] + wide[:, 8 + h : 9 + h]

    queries = dqg[...].reshape(512, 512)
    keys = kv[8:12].reshape(512, 512)
    lse_list = []
    for h in range(4):
        g = h // 2
        scores = dot(
            queries[:, h * HD : (h + 1) * HD], keys[:, g * HD : (g + 1) * HD], ((1,), (1,))
        )
        scores = scores * SCORE_SCALE + bias
        top = jnp.max(scores, axis=1, keepdims=True)
        weights_h = jnp.exp(scores - top)
        total = jnp.sum(weights_h, axis=1, keepdims=True)
        mixed = dot(
            weights_h.astype(BF16), keys[:, 256 + g * HD : 256 + (g + 1) * HD], ((1,), (0,))
        )
        dpart[:, :, h * HD : (h + 1) * HD] = (mixed / total).astype(BF16).reshape(32, 16, HD)
        lse_list.append(top + jnp.log(total))
    dpart[:, :, 512:640] = pack(lse_list).reshape(32, 16, 128)

    def r1(j, slot_y, target_y):
        return pltpu.make_async_remote_copy(
            src_ref=dpart.at[pl.ds(lax.rem(target_y + NY, NY) * NZ, NZ)],
            dst_ref=b1.at[lax.rem(slot_y + NY, NY)],
            send_sem=r1_send.at[j - 1], recv_sem=r1_recv.at[j - 1],
            device_id=(ctx_of(target_y, z), me_t), device_id_type=MESH,
        )

    def r2(j, slot_z, target_z):
        return pltpu.make_async_remote_copy(
            src_ref=p2.at[lax.rem(target_z + NZ, NZ)],
            dst_ref=b2.at[lax.rem(slot_z + NZ, NZ)],
            send_sem=r2_send.at[j - 1], recv_sem=r2_recv.at[j - 1],
            device_id=(ctx_of(y, target_z), me_t), device_id_type=MESH,
        )

    for j in range(1, NY):
        r1(j, y, y + j).start()
    b1[y] = dpart[pl.ds(y * NZ, NZ)]

    for s in range(NCH):
        halo(0, s).wait_recv()
        halo(2, s).wait_recv()
    width = WINDOW + CH
    rows2 = lax.rem(lax.broadcasted_iota(jnp.int32, (2 * CH, 1), 0), CH)
    cols = lax.broadcasted_iota(jnp.int32, (1, CH), 1)
    columns = lax.broadcasted_iota(jnp.int32, (1, width), 1)

    def attend(i, carry):
        low = jnp.where(columns >= (2 - block) * 512 - i * CH, 0.0, NEG)
        alive = block * 512 + i * CH + rows2 < length
        for g in range(2):
            query = jnp.concatenate(
                [q_s[i, :, (2 * g + r) * HD : (2 * g + r + 1) * HD] for r in range(2)], axis=0
            )
            window = kv[pl.ds(i, 9)].reshape(width, 512)
            scores = dot(query, window[:, g * HD : (g + 1) * HD], ((1,), (1,)))
            scores = scores * SCORE_SCALE + low
            scores = jnp.concatenate(
                [
                    jnp.where(cols > rows2, scores[:, :CH], NEG),
                    scores[:, CH:WINDOW],
                    jnp.where(cols <= rows2, scores[:, WINDOW:], NEG),
                ],
                axis=1,
            )
            top = jnp.max(scores, axis=1, keepdims=True)
            weights_h = jnp.exp(scores - top)
            total = jnp.sum(weights_h, axis=1, keepdims=True)
            mixed = dot(
                weights_h.astype(BF16),
                window[:, 256 + g * HD : 256 + (g + 1) * HD],
                ((1,), (0,)),
            )
            mixed = jnp.where(alive, mixed / total, 0.0).astype(BF16)
            for r in range(2):
                out_ref[
                    pl.ds(pl.multiple_of(i * CH, CH), CH),
                    (2 * g + r) * HD : (2 * g + r + 1) * HD,
                ] = mixed[r * CH : (r + 1) * CH]
        return carry

    lax.fori_loop(0, NCH, attend, 0)

    for j in range(1, NY):
        r1(j, y - j, y).wait_recv()

    def merge(parts, masks, h):
        lses = [lse_of(part[:, 512:640], h) for part in parts]
        if masks is not None:
            lses = [jnp.where(mask, lse, NEG) for mask, lse in zip(masks, lses)]
        top = functools.reduce(jnp.maximum, lses)
        factors = [jnp.exp(lse - top) for lse in lses]
        total = sum(factors)
        mixed = sum(
            f * part[:, h * HD : (h + 1) * HD].astype(F32) for f, part in zip(factors, parts)
        )
        return top, total, mixed

    parts = [b1[i].reshape(128, 640) for i in range(NY)]
    lse_list = []
    for h in range(4):
        top, total, mixed = merge(parts, None, h)
        p2[:, :, h * HD : (h + 1) * HD] = (mixed / total).astype(BF16).reshape(8, 16, HD)
        lse_list.append(top + jnp.log(total))
    p2[:, :, 512:640] = pack(lse_list).reshape(8, 16, 128)
    for j in range(1, NZ):
        r2(j, z, z + j).start()
    b2[z] = p2[z]
    for j in range(1, NZ):
        r2(j, z - j, z).wait_recv()
    parts = [b2[i] for i in range(NZ)]
    masks = [rp[:, :1] == i % PROMPTS for i in range(NZ)]
    own_query = dqg[me_c].astype(F32)
    for h in range(4):
        g = h // 2
        top, total, mixed = merge(parts, masks, h)
        own = (
            jnp.sum(
                own_query[:, h * HD : (h + 1) * HD]
                * dk_s[:, g * HD : (g + 1) * HD].astype(F32),
                axis=1,
                keepdims=True,
            )
            * SCORE_SCALE
        )
        new_top = jnp.maximum(top, own)
        shift = jnp.exp(top - new_top)
        weight = jnp.exp(own - new_top)
        value = dv_s[:, g * HD : (g + 1) * HD].astype(F32)
        dout_ref[:, h * HD : (h + 1) * HD] = (
            (mixed * shift + weight * value) / (total * shift + weight)
        ).astype(BF16)

    for k in range(6):
        ag_sent(k)
    for s in range(NCH):
        for kind in range(3):
            halo(kind, s).wait_send()
    for j in range(1, NZ):
        dq1(j, z, z + j).wait_send()
        r2(j, z, z + j).wait_send()
    for j in range(1, NY):
        dq2(j, y, y + j).wait_send()
        r1(j, y, y + j).wait_send()


def local(
    prompt_states,
    decode_states,
    norm_gain,
    query_weight,
    key_weight,
    value_weight,
    query_gain,
    key_gain,
    prompt_lengths,
    row_prompt,
):
    tok_rows, feat = prompt_states.shape
    dec_rows = decode_states.shape[0]
    feature_count = norm_gain.shape[0]
    half = HD // 2
    mine = lax.dynamic_slice(norm_gain, (lax.axis_index("tp") * feat,), (feat,))
    gain_column = jnp.broadcast_to(mine[:, None], (feat, 128))
    frequency = np.array([10000.0 ** (-2.0 * (j % half) / HD) for j in range(HD)], np.float32)
    sign = np.array([-1.0] * half + [1.0] * half, np.float32)
    rows = jnp.broadcast_to(row_prompt[:, None], (dec_rows, 128))
    vmem = pl.BlockSpec(memory_space=pltpu.VMEM)
    hbm = pl.BlockSpec(memory_space=pl.ANY)
    dma = pltpu.SemaphoreType.DMA
    return pl.pallas_call(
        functools.partial(kernel, float(feature_count)),
        out_shape=(
            jax.ShapeDtypeStruct((tok_rows, 512), BF16),
            jax.ShapeDtypeStruct((dec_rows, 512), BF16),
        ),
        in_specs=[vmem] * 9 + [pl.BlockSpec(memory_space=pltpu.SMEM)] + [hbm] * 3,
        out_specs=(vmem, vmem),
        scratch_shapes=[
            pltpu.VMEM((NCH, 8, feat, CH), BF16),
            pltpu.VMEM((8, dec_rows, feat), BF16),
            pltpu.VMEM((8, 6, 8, 128), F32),
            pltpu.VMEM((feature_count, 512), BF16),
            pltpu.VMEM((feature_count, 512), BF16),
            pltpu.VMEM((12, CH, 512), BF16),
            pltpu.VMEM((NCH, CH, 512), BF16),
            pltpu.VMEM((NCH, CH, 512), BF16),
            pltpu.VMEM((32, dec_rows, 512), BF16),
            pltpu.VMEM((dec_rows, 256), BF16),
            pltpu.VMEM((dec_rows, 256), BF16),
            pltpu.VMEM((32, dec_rows, 640), BF16),
            pltpu.VMEM((NY, NZ, dec_rows, 640), BF16),
            pltpu.VMEM((NZ, dec_rows, 640), BF16),
            pltpu.VMEM((NZ, dec_rows, 640), BF16),
            dma((6, 7)), dma((6, 7)), dma((3,)), dma((3, NCH)), dma((3, NCH)),
            dma((NZ - 1,)), dma((NZ - 1,)), dma((NY - 1,)), dma((NY - 1,)),
            dma((NY - 1,)), dma((NY - 1,)), dma((NZ - 1,)), dma((NZ - 1,)),
        ],
        compiler_params=pltpu.CompilerParams(
            collective_id=0, has_side_effects=True, vmem_limit_bytes=60 * 2**20
        ),
    )(
        prompt_states.T,
        decode_states,
        gain_column,
        mine[None, :],
        rows,
        jnp.asarray(frequency)[None, :],
        jnp.asarray(sign)[None, :],
        query_gain[None, :],
        key_gain[None, :],
        prompt_lengths,
        query_weight,
        key_weight,
        value_weight,
    )


def solution(mesh):
    placed = (
        P("ctx", "tp"),
        P("ctx", "tp"),
        P(),
        P(None, "tp"),
        P(None, "tp"),
        P(None, "tp"),
        P(),
        P(),
        P(),
        P("ctx"),
    )
    return jax.shard_map(
        local,
        mesh=mesh,
        in_specs=placed,
        out_specs=(P("ctx", "tp"), P("ctx", "tp")),
        check_vma=False,
    )
```

```python
import functools
import math

import jax
import jax.numpy as jnp
import numpy as np
from jax import lax
from jax.experimental import pallas as pl
from jax.experimental.pallas import tpu as pltpu
from jax.sharding import PartitionSpec as P

MESH = pl.DeviceIdType.MESH
F32, BF16 = jnp.float32, jnp.bfloat16
WINDOW = 1024
PROMPTS = 4
EPS = 1e-06
SCORE_SCALE = 168.0 ** (-0.5)
HD = 128
NY, NZ, NX = 4, 8, 4
CH = 128
NCH = 4
NEG = -1e30


def dot(a, b, dims):
    return lax.dot_general(a, b, (dims, ((), ())), preferred_element_type=F32)


def kernel(
    feature_count,
    x_ref, xd_ref, gain_ref, freq_ref, sgn_ref, qg_ref, kg_ref, len_ref, rp_ref,
    wq_hbm, wk_hbm, wv_hbm,
    out_ref, dout_ref,
    xg, xd, ss, wkv, wq, kv, q_s, dqg, dk_s, dv_s, dpart, b1, p2, b2, top_s, sum_s, mix_s,
    ag_send, ag_recv, wsem, h_send, h_recv,
    dq1_send, dq1_recv, dq2_send, dq2_recv, r1_send, r1_recv, r2_send, r2_recv,
):
    me_c = lax.axis_index("ctx")
    me_t = lax.axis_index("tp")
    x, c = me_t // 2, lax.rem(me_t, 2)
    y, z = me_c // NZ, lax.rem(me_c, NZ)
    way = 1 - 2 * c
    feat = x_ref.shape[0]
    block = 2 * y + z // 4
    prompt = lax.rem(z, PROMPTS)

    def tp_of(xx, cc):
        return lax.rem(xx + NX, NX) * 2 + cc

    def ctx_of(yy, zz):
        return lax.rem(yy + NY, NY) * NZ + lax.rem(zz + NZ, NZ)

    near_a, near_b, far = tp_of(x - way, c), tp_of(x + way, c), tp_of(x + 2, c)
    partner = tp_of(x, 1 - c)
    from_partner = (partner, tp_of(x + way, 1 - c), tp_of(x - way, 1 - c), tp_of(x + 2, 1 - c))
    out_b1 = ctx_of(y + z // 4, z + 4)
    in_b1 = ctx_of(y - (1 - z // 4), z + 4)

    weights = (
        pltpu.make_async_copy(wk_hbm, wkv.at[:, 0:256], wsem.at[0]),
        pltpu.make_async_copy(wv_hbm, wkv.at[:, 256:512], wsem.at[1]),
        pltpu.make_async_copy(wq_hbm, wq, wsem.at[2]),
    )
    for copy in weights:
        copy.start()

    barrier = pltpu.get_barrier_semaphore()
    for device in (
        [(me_c, t) for t in (near_a, near_b, far, partner)]
        + [(ctx_of(y, z + j), me_t) for j in range(1, NZ)]
        + [(ctx_of(y + j, z), me_t) for j in range(1, NY)]
        + [(in_b1, me_t)]
    ):
        pl.semaphore_signal(barrier, inc=1, device_id=device, device_id_type=MESH)

    gain_row = gain_ref[:, 0:feat]
    for t in range(1, 8):
        gain_row = jnp.where(me_t == t, gain_ref[:, t * feat : (t + 1) * feat], gain_row)
    gain_column = jnp.transpose(jnp.broadcast_to(gain_row, (128, feat)))
    decode_wide = xd_ref[...].astype(F32)
    xd[me_t] = (decode_wide * gain_row).astype(BF16)
    decode_sum = jnp.sum(decode_wide * decode_wide, axis=1, keepdims=True)
    ss[me_t, 4:6] = jnp.broadcast_to(decode_sum, (16, 128)).reshape(2, 8, 128)
    for k in range(NCH):
        wide = x_ref[:, k * CH : (k + 1) * CH].astype(F32)
        xg[k, me_t] = (wide * gain_column).astype(BF16)
        ss[me_t, k] = jnp.sum((wide * wide).reshape(feat // 8, 8, CH), axis=0)

    pl.semaphore_wait(barrier, 15)

    def piece(k, d):
        if isinstance(k, int) and k == 4:
            return xd.at[d]
        if isinstance(k, int) and k == 5:
            return ss.at[d]
        return xg.at[k, d]

    def ag(k, d, j, target):
        return pltpu.make_async_remote_copy(
            src_ref=piece(k, d), dst_ref=piece(k, d),
            send_sem=ag_send.at[k, j], recv_sem=ag_recv.at[k, j],
            device_id=(me_c, target), device_id_type=MESH,
        )

    def start_own(k):
        ag(k, me_t, 0, near_b).start()
        ag(k, me_t, 1, near_a).start()
        ag(k, me_t, 2, far).start()
        ag(k, me_t, 3, partner).start()

    def gather(k):
        for j, d in enumerate((near_a, near_b, far)):
            ag(k, d, j, near_b).wait_recv()
            ag(k, d, 4 + j, partner).start()
        for j in range(4):
            ag(k, from_partner[j], 3 + j, near_b).wait_recv()

    def ag_sent(k):
        for j in range(7):
            ag(k, me_t, j, near_b).wait_send()

    def halo(kind, s):
        slot, target = ((4 + s, ctx_of(y + 1, z)), (s, out_b1))[kind]
        return pltpu.make_async_remote_copy(
            src_ref=kv.at[8 + s], dst_ref=kv.at[slot],
            send_sem=h_send.at[kind, s], recv_sem=h_recv.at[kind, s],
            device_id=(target, me_t), device_id_type=MESH,
        )

    freq, sgn = freq_ref[...], sgn_ref[...]

    def rope_tables(positions):
        angles = positions * freq
        return jnp.cos(angles), jnp.sin(angles) * sgn

    def head(acc, gain, tables):
        unit = acc * lax.rsqrt(jnp.mean(acc * acc, axis=1, keepdims=True) + EPS) * gain
        return (unit * tables[0] + pltpu.roll(unit, HD // 2, axis=1) * tables[1]).astype(BF16)

    qg, kg = qg_ref[...], kg_ref[...]

    for k in (5, 4, 0, 1, 2, 3):
        start_own(k)
    for k in (5, 4):
        gather(k)

    for copy in weights:
        copy.wait()
    acc_kv = jnp.zeros((16, 512), F32)
    acc_q = jnp.zeros((16, 512), F32)
    for d in range(8):
        rows = slice(d * feat, (d + 1) * feat)
        acc_kv += dot(xd[d], wkv[rows, :], ((1,), (0,)))
        acc_q += dot(xd[d], wq[rows, :], ((1,), (0,)))
    rows16 = lax.broadcasted_iota(jnp.int32, (16, 128), 0)
    rp = jnp.zeros((16, 128), jnp.int32)
    for r in range(16):
        rp = jnp.where(rows16 == r, rp_ref[r], rp)
    decode_pos = jnp.zeros((16, 128), jnp.int32)
    for p in range(PROMPTS):
        decode_pos = jnp.where(rp == p, len_ref[p], decode_pos)
    tables = rope_tables(decode_pos.astype(F32))
    sums = jnp.sum(ss[:, 4:6], axis=0).reshape(16, 128)
    inverse = lax.rsqrt(sums / feature_count + EPS)
    for h in range(4):
        dqg[me_c, :, h * HD : (h + 1) * HD] = head(
            acc_q[:, h * HD : (h + 1) * HD] * inverse, qg, tables
        )
    for h in range(2):
        dk_s[:, h * HD : (h + 1) * HD] = head(
            acc_kv[:, h * HD : (h + 1) * HD] * inverse, kg, tables
        )
        dv_s[:, h * HD : (h + 1) * HD] = (
            acc_kv[:, 256 + h * HD : 256 + (h + 1) * HD] * inverse
        ).astype(BF16)

    def dq1(j, owner_z, target_z):
        slot = dqg.at[ctx_of(y, owner_z)]
        return pltpu.make_async_remote_copy(
            src_ref=slot, dst_ref=slot, send_sem=dq1_send.at[j - 1], recv_sem=dq1_recv.at[j - 1],
            device_id=(ctx_of(y, target_z), me_t), device_id_type=MESH,
        )

    def dq2(j, owner_y, target_y):
        slots = dqg.at[pl.ds(lax.rem(owner_y + NY, NY) * NZ, NZ)]
        return pltpu.make_async_remote_copy(
            src_ref=slots, dst_ref=slots, send_sem=dq2_send.at[j - 1], recv_sem=dq2_recv.at[j - 1],
            device_id=(ctx_of(target_y, z), me_t), device_id_type=MESH,
        )

    for j in range(1, NZ):
        dq1(j, z, z + j).start()

    row_index = lax.broadcasted_iota(jnp.int32, (CH, 1), 0)

    def project(s, carry):
        gather(s)
        states = xg[s].reshape(8 * feat, CH)
        sums = jnp.sum(jnp.transpose(jnp.sum(ss[:, s], axis=0)), axis=1, keepdims=True)
        inverse = lax.rsqrt(sums / feature_count + EPS)
        tables = rope_tables((block * 512 + s * CH + row_index).astype(F32))
        acc = dot(states, wkv[...], ((0,), (0,)))
        for h in range(2):
            kv[8 + s, :, h * HD : (h + 1) * HD] = head(
                acc[:, h * HD : (h + 1) * HD] * inverse, kg, tables
            )
        kv[8 + s, :, 256:512] = (acc[:, 256:512] * inverse).astype(BF16)
        halo(0, s).start()
        halo(1, s).start()
        acc = dot(states, wq[...], ((0,), (0,)))
        for h in range(4):
            q_s[s, :, h * HD : (h + 1) * HD] = head(
                acc[:, h * HD : (h + 1) * HD] * inverse, qg, tables
            )

        @pl.when(s == 1)
        def _():
            for j in range(1, NZ):
                dq1(j, z - j, z).wait_recv()
            for j in range(1, NY):
                dq2(j, y, y + j).start()

        return carry

    lax.fori_loop(0, NCH, project, 0)

    for j in range(1, NY):
        dq2(j, y - j, y).wait_recv()
    length = len_ref[prompt]
    key_pos = block * 512 + lax.broadcasted_iota(jnp.int32, (1, 512), 1)
    bias = jnp.where((key_pos >= length - WINDOW) & (key_pos < length), 0.0, NEG)
    lane = lax.broadcasted_iota(jnp.int32, (1, 128), 1)

    def pack(lse_list):
        packed = None
        for h, lse in enumerate(lse_list):
            high = lse.astype(BF16).astype(F32)
            middle = (lse - high).astype(BF16).astype(F32)
            low = lse - high - middle
            term = (
                jnp.where(lane == h, high, 0.0)
                + jnp.where(lane == 4 + h, middle, 0.0)
                + jnp.where(lane == 8 + h, low, 0.0)
            )
            packed = term if packed is None else packed + term
        return packed.astype(BF16)

    def lse_of(packed, h):
        wide = packed.astype(F32)
        return wide[:, h : h + 1] + wide[:, 4 + h : 5 + h] + wide[:, 8 + h : 9 + h]

    queries = dqg[...].reshape(512, 512)
    keys = kv[8:12].reshape(512, 512)
    lse_list = []
    for h in range(4):
        g = h // 2
        scores = dot(
            queries[:, h * HD : (h + 1) * HD], keys[:, g * HD : (g + 1) * HD], ((1,), (1,))
        )
        scores = scores * SCORE_SCALE + bias
        top = jnp.max(scores, axis=1, keepdims=True)
        weights_h = jnp.exp(scores - top)
        total = jnp.sum(weights_h, axis=1, keepdims=True)
        mixed = dot(
            weights_h.astype(BF16), keys[:, 256 + g * HD : 256 + (g + 1) * HD], ((1,), (0,))
        )
        dpart[:, :, h * HD : (h + 1) * HD] = (mixed / total).astype(BF16).reshape(32, 16, HD)
        lse_list.append(top + jnp.log(total))
    dpart[:, :, 512:640] = pack(lse_list).reshape(32, 16, 128)

    def r1(j, slot_y, target_y):
        return pltpu.make_async_remote_copy(
            src_ref=dpart.at[pl.ds(lax.rem(target_y + NY, NY) * NZ, NZ)],
            dst_ref=b1.at[lax.rem(slot_y + NY, NY)],
            send_sem=r1_send.at[j - 1], recv_sem=r1_recv.at[j - 1],
            device_id=(ctx_of(target_y, z), me_t), device_id_type=MESH,
        )

    def r2(j, slot_z, target_z):
        return pltpu.make_async_remote_copy(
            src_ref=p2.at[lax.rem(target_z + NZ, NZ)],
            dst_ref=b2.at[lax.rem(slot_z + NZ, NZ)],
            send_sem=r2_send.at[j - 1], recv_sem=r2_recv.at[j - 1],
            device_id=(ctx_of(y, target_z), me_t), device_id_type=MESH,
        )

    for j in range(1, NY):
        r1(j, y, y + j).start()
    b1[y] = dpart[pl.ds(y * NZ, NZ)]

    def query_of(i, g):
        return jnp.concatenate(
            [q_s[i, :, (2 * g + r) * HD : (2 * g + r + 1) * HD] for r in range(2)], axis=0
        )

    def softmax(scores, window, g):
        top = jnp.max(scores, axis=1, keepdims=True)
        weights_h = jnp.exp(scores - top)
        total = jnp.sum(weights_h, axis=1, keepdims=True)
        values = window[:, 256 + g * HD : 256 + (g + 1) * HD]
        return top, total, dot(weights_h.astype(BF16), values, ((1,), (0,)))

    for s in range(NCH):
        halo(0, s).wait_recv()
    width = 5 * CH
    rows2 = lax.rem(lax.broadcasted_iota(jnp.int32, (2 * CH, 1), 0), CH)
    cols = lax.broadcasted_iota(jnp.int32, (1, CH), 1)
    columns = lax.broadcasted_iota(jnp.int32, (1, width), 1)

    def attend_first(i, carry):
        low = jnp.where((block >= 2) | (columns >= (4 - i) * CH), 0.0, NEG)
        for g in range(2):
            window = kv[pl.ds(4 + i, 5)].reshape(width, 512)
            scores = dot(query_of(i, g), window[:, g * HD : (g + 1) * HD], ((1,), (1,)))
            scores = scores * SCORE_SCALE + low
            scores = jnp.concatenate(
                [
                    jnp.where(cols > rows2, scores[:, :CH], NEG),
                    scores[:, CH : 4 * CH],
                    jnp.where(cols <= rows2, scores[:, 4 * CH :], NEG),
                ],
                axis=1,
            )
            top, total, mixed = softmax(scores, window, g)
            top_s[i, g], sum_s[i, g], mix_s[i, g] = top, total, mixed
        return carry

    lax.fori_loop(0, NCH, attend_first, 0)
    for s in range(NCH):
        halo(1, s).wait_recv()
    absent = jnp.where(block == 0, NEG, 0.0)

    def attend_last(i, carry):
        alive = block * 512 + i * CH + rows2 < length
        for g in range(2):
            window = kv[0:4].reshape(512, 512)
            scores = dot(query_of(i, g), window[:, g * HD : (g + 1) * HD], ((1,), (1,)))
            top, total, mixed = softmax(scores * SCORE_SCALE + absent, window, g)
            first_top = top_s[i, g]
            both = jnp.maximum(top, first_top)
            f1, f2 = jnp.exp(first_top - both), jnp.exp(top - both)
            mixed = (mix_s[i, g] * f1 + mixed * f2) / (sum_s[i, g] * f1 + total * f2)
            mixed = jnp.where(alive, mixed, 0.0).astype(BF16)
            for r in range(2):
                out_ref[
                    pl.ds(pl.multiple_of(i * CH, CH), CH),
                    (2 * g + r) * HD : (2 * g + r + 1) * HD,
                ] = mixed[r * CH : (r + 1) * CH]
        return carry

    lax.fori_loop(0, NCH, attend_last, 0)

    for j in range(1, NY):
        r1(j, y - j, y).wait_recv()

    def merge(parts, masks, h):
        lses = [lse_of(part[:, 512:640], h) for part in parts]
        if masks is not None:
            lses = [jnp.where(mask, lse, NEG) for mask, lse in zip(masks, lses)]
        top = functools.reduce(jnp.maximum, lses)
        factors = [jnp.exp(lse - top) for lse in lses]
        total = sum(factors)
        mixed = sum(
            f * part[:, h * HD : (h + 1) * HD].astype(F32) for f, part in zip(factors, parts)
        )
        return top, total, mixed

    parts = [b1[i].reshape(128, 640) for i in range(NY)]
    lse_list = []
    for h in range(4):
        top, total, mixed = merge(parts, None, h)
        p2[:, :, h * HD : (h + 1) * HD] = (mixed / total).astype(BF16).reshape(8, 16, HD)
        lse_list.append(top + jnp.log(total))
    p2[:, :, 512:640] = pack(lse_list).reshape(8, 16, 128)
    for j in range(1, NZ):
        r2(j, z, z + j).start()
    b2[z] = p2[z]
    for j in range(1, NZ):
        r2(j, z - j, z).wait_recv()
    parts = [b2[i] for i in range(NZ)]
    masks = [rp[:, :1] == i % PROMPTS for i in range(NZ)]
    own_query = dqg[me_c].astype(F32)
    for h in range(4):
        g = h // 2
        top, total, mixed = merge(parts, masks, h)
        own = (
            jnp.sum(
                own_query[:, h * HD : (h + 1) * HD]
                * dk_s[:, g * HD : (g + 1) * HD].astype(F32),
                axis=1,
                keepdims=True,
            )
            * SCORE_SCALE
        )
        new_top = jnp.maximum(top, own)
        shift = jnp.exp(top - new_top)
        weight = jnp.exp(own - new_top)
        value = dv_s[:, g * HD : (g + 1) * HD].astype(F32)
        dout_ref[:, h * HD : (h + 1) * HD] = (
            (mixed * shift + weight * value) / (total * shift + weight)
        ).astype(BF16)

    for k in range(6):
        ag_sent(k)
    for s in range(NCH):
        for kind in range(2):
            halo(kind, s).wait_send()
    for j in range(1, NZ):
        dq1(j, z, z + j).wait_send()
        r2(j, z, z + j).wait_send()
    for j in range(1, NY):
        dq2(j, y, y + j).wait_send()
        r1(j, y, y + j).wait_send()


def hand_over(a_ref, b_ref, a_out, b_out):
    a_out[...] = a_ref[...]
    b_out[...] = b_ref[...]


def local(
    prompt_states,
    decode_states,
    norm_gain,
    query_weight,
    key_weight,
    value_weight,
    query_gain,
    key_gain,
    prompt_lengths,
    row_prompt,
):
    tok_rows, feat = prompt_states.shape
    dec_rows = decode_states.shape[0]
    feature_count = norm_gain.shape[0]
    half = HD // 2
    frequency = np.array([10000.0 ** (-2.0 * (j % half) / HD) for j in range(HD)], np.float32)
    sign = np.array([-1.0] * half + [1.0] * half, np.float32)
    vmem = pl.BlockSpec(memory_space=pltpu.VMEM)
    hbm = pl.BlockSpec(memory_space=pl.ANY)
    dma = pltpu.SemaphoreType.DMA
    attended = pl.pallas_call(
        functools.partial(kernel, float(feature_count)),
        out_shape=(
            jax.ShapeDtypeStruct((tok_rows, 512), BF16),
            jax.ShapeDtypeStruct((dec_rows, 512), BF16),
        ),
        in_specs=[vmem] * 7 + [pl.BlockSpec(memory_space=pltpu.SMEM)] * 2 + [hbm] * 3,
        out_specs=(vmem, vmem),
        scratch_shapes=[
            pltpu.VMEM((NCH, 8, feat, CH), BF16),
            pltpu.VMEM((8, dec_rows, feat), BF16),
            pltpu.VMEM((8, 6, 8, 128), F32),
            pltpu.VMEM((feature_count, 512), BF16),
            pltpu.VMEM((feature_count, 512), BF16),
            pltpu.VMEM((12, CH, 512), BF16),
            pltpu.VMEM((NCH, CH, 512), BF16),
            pltpu.VMEM((32, dec_rows, 512), BF16),
            pltpu.VMEM((dec_rows, 256), BF16),
            pltpu.VMEM((dec_rows, 256), BF16),
            pltpu.VMEM((32, dec_rows, 640), BF16),
            pltpu.VMEM((NY, NZ, dec_rows, 640), BF16),
            pltpu.VMEM((NZ, dec_rows, 640), BF16),
            pltpu.VMEM((NZ, dec_rows, 640), BF16),
            pltpu.VMEM((NCH, 2, 2 * CH, 1), F32),
            pltpu.VMEM((NCH, 2, 2 * CH, 1), F32),
            pltpu.VMEM((NCH, 2, 2 * CH, HD), F32),
            dma((6, 7)), dma((6, 7)), dma((3,)), dma((2, NCH)), dma((2, NCH)),
            dma((NZ - 1,)), dma((NZ - 1,)), dma((NY - 1,)), dma((NY - 1,)),
            dma((NY - 1,)), dma((NY - 1,)), dma((NZ - 1,)), dma((NZ - 1,)),
        ],
        compiler_params=pltpu.CompilerParams(
            collective_id=0, has_side_effects=True, vmem_limit_bytes=60 * 2**20
        ),
    )(
        prompt_states.T,
        decode_states,
        norm_gain[None, :],
        jnp.asarray(frequency)[None, :],
        jnp.asarray(sign)[None, :],
        query_gain[None, :],
        key_gain[None, :],
        prompt_lengths,
        row_prompt,
        query_weight,
        key_weight,
        value_weight,
    )
    return pl.pallas_call(
        hand_over,
        out_shape=tuple(jax.ShapeDtypeStruct(a.shape, a.dtype) for a in attended),
        in_specs=[vmem] * 2,
        out_specs=(vmem, vmem),
    )(*attended)


def solution(mesh):
    placed = (
        P("ctx", "tp"),
        P("ctx", "tp"),
        P(),
        P(None, "tp"),
        P(None, "tp"),
        P(None, "tp"),
        P(),
        P(),
        P(),
        P("ctx"),
    )
    return jax.shard_map(
        local,
        mesh=mesh,
        in_specs=placed,
        out_specs=(P("ctx", "tp"), P("ctx", "tp")),
        check_vma=False,
    )
```

```python
import functools
import math

import jax
import jax.numpy as jnp
import numpy as np
from jax import lax
from jax.experimental import pallas as pl
from jax.experimental.pallas import tpu as pltpu
from jax.sharding import PartitionSpec as P

MESH = pl.DeviceIdType.MESH
F32, BF16 = jnp.float32, jnp.bfloat16
WINDOW = 1024
PROMPTS = 4
EPS = 1e-06
SCORE_SCALE = 168.0 ** (-0.5)
LOG2_SCALE = SCORE_SCALE * math.log2(math.e)
HD = 128
NY, NZ, NX = 4, 8, 4
CH = 128
NCH = 4
NEG = -1e30


def dot(a, b, dims):
    return lax.dot_general(a, b, (dims, ((), ())), preferred_element_type=F32)


def kernel(
    feature_count,
    x_ref, xd_ref, gain_ref, freq_ref, sgn_ref, qg_ref, kg_ref, len_ref, rp_ref,
    wq_hbm, wk_hbm, wv_hbm,
    out_ref, dout_ref,
    xg, xd, ss, wkv, wq, kv, q_s, dqg, dk_s, dv_s, dpart, b1, p2, b2, top_s, sum_s, mix_s, gain_s,
    ag_send, ag_recv, wsem, h_send, h_recv,
    dq1_send, dq1_recv, dq2_send, dq2_recv, r1_send, r1_recv, r2_send, r2_recv,
):
    me_c = lax.axis_index("ctx")
    me_t = lax.axis_index("tp")
    x, c = me_t // 2, lax.rem(me_t, 2)
    y, z = me_c // NZ, lax.rem(me_c, NZ)
    way = 1 - 2 * c
    feat = x_ref.shape[0]
    block = 2 * y + z // 4
    prompt = lax.rem(z, PROMPTS)

    def tp_of(xx, cc):
        return lax.rem(xx + NX, NX) * 2 + cc

    def ctx_of(yy, zz):
        return lax.rem(yy + NY, NY) * NZ + lax.rem(zz + NZ, NZ)

    near_a, near_b, far = tp_of(x - way, c), tp_of(x + way, c), tp_of(x + 2, c)
    partner = tp_of(x, 1 - c)
    from_partner = (partner, tp_of(x + way, 1 - c), tp_of(x - way, 1 - c), tp_of(x + 2, 1 - c))
    out_b1 = ctx_of(y + z // 4, z + 4)
    in_b1 = ctx_of(y - (1 - z // 4), z + 4)

    weights = (
        pltpu.make_async_copy(wk_hbm, wkv.at[:, 0:256], wsem.at[0]),
        pltpu.make_async_copy(wv_hbm, wkv.at[:, 256:512], wsem.at[1]),
        pltpu.make_async_copy(wq_hbm, wq, wsem.at[2]),
    )
    for copy in weights:
        copy.start()

    barrier = pltpu.get_barrier_semaphore()
    for device in (
        [(me_c, t) for t in (near_a, near_b, partner)]
        + [(ctx_of(y, z + j), me_t) for j in range(1, NZ)]
        + [(ctx_of(y + j, z), me_t) for j in range(1, NY)]
        + [(in_b1, me_t)]
    ):
        pl.semaphore_signal(barrier, inc=1, device_id=device, device_id_type=MESH)

    gains = gain_ref.shape[0]
    padded = jnp.concatenate([gain_ref[...], jnp.zeros((128 - gains, 128), F32)], axis=0)
    columns_of = jnp.transpose(padded)
    for r in range(gains):
        gain_s[r * 128 : (r + 1) * 128] = jnp.broadcast_to(columns_of[:, r : r + 1], (128, 128))
    gain_column = gain_s[pl.ds(pl.multiple_of(me_t * feat, 32), feat), :]
    gain_row = jnp.transpose(
        jnp.concatenate([gain_column, jnp.zeros((-feat % 128, 128), F32)], axis=0)
    )[0:1, :feat]
    decode_wide = xd_ref[...].astype(F32)
    xd[me_t] = (decode_wide * gain_row).astype(BF16)
    decode_sum = jnp.sum(decode_wide * decode_wide, axis=1, keepdims=True)
    ss[me_t, 4:6] = jnp.broadcast_to(decode_sum, (16, 128)).reshape(2, 8, 128)
    for k in range(NCH):
        wide = x_ref[:, k * CH : (k + 1) * CH].astype(F32)
        xg[k, me_t] = (wide * gain_column).astype(BF16)
        ss[me_t, k] = jnp.sum((wide * wide).reshape(feat // 8, 8, CH), axis=0)

    pl.semaphore_wait(barrier, 14)

    def piece(k, d):
        if isinstance(k, int) and k == 4:
            return xd.at[d]
        if isinstance(k, int) and k == 5:
            return ss.at[d]
        return xg.at[k, d]

    def ag(k, d, j, target):
        return pltpu.make_async_remote_copy(
            src_ref=piece(k, d), dst_ref=piece(k, d),
            send_sem=ag_send.at[k, j], recv_sem=ag_recv.at[k, j],
            device_id=(me_c, target), device_id_type=MESH,
        )

    def start_own(k):
        ag(k, me_t, 0, near_b).start()
        ag(k, me_t, 1, near_a).start()
        ag(k, me_t, 3, partner).start()

    def take(k):
        ag(k, near_a, 0, near_b).wait_recv()
        ag(k, near_a, 2, near_b).start()
        ag(k, near_a, 4, partner).start()
        ag(k, near_b, 1, near_b).wait_recv()
        ag(k, near_b, 5, partner).start()

    def finish(k):
        ag(k, far, 2, near_b).wait_recv()
        ag(k, far, 6, partner).start()
        for j in range(4):
            ag(k, from_partner[j], 3 + j, near_b).wait_recv()

    def ag_sent(k):
        for j in range(7):
            ag(k, me_t, j, near_b).wait_send()

    def halo(kind, s):
        slot, target = ((4 + s, ctx_of(y + 1, z)), (s, out_b1))[kind]
        return pltpu.make_async_remote_copy(
            src_ref=kv.at[8 + s], dst_ref=kv.at[slot],
            send_sem=h_send.at[kind, s], recv_sem=h_recv.at[kind, s],
            device_id=(target, me_t), device_id_type=MESH,
        )

    freq, sgn = freq_ref[...], sgn_ref[...]

    def rope_tables(positions):
        angles = positions * freq
        return jnp.cos(angles), jnp.sin(angles) * sgn

    def head(acc, gain, tables):
        unit = acc * lax.rsqrt(jnp.mean(acc * acc, axis=1, keepdims=True) + EPS) * gain
        return (unit * tables[0] + pltpu.roll(unit, HD // 2, axis=1) * tables[1]).astype(BF16)

    qg, kg = qg_ref[...], kg_ref[...]

    for k in (5, 4, 0, 1):
        start_own(k)
    for k in (5, 4, 0):
        take(k)
    start_own(2)
    for k in (5, 4):
        finish(k)

    for copy in weights:
        copy.wait()
    acc_kv = jnp.zeros((16, 512), F32)
    acc_q = jnp.zeros((16, 512), F32)
    for d in range(8):
        rows = slice(d * feat, (d + 1) * feat)
        acc_kv += dot(xd[d], wkv[rows, :], ((1,), (0,)))
        acc_q += dot(xd[d], wq[rows, :], ((1,), (0,)))
    rows16 = lax.broadcasted_iota(jnp.int32, (16, 128), 0)
    rp = jnp.zeros((16, 128), jnp.int32)
    for r in range(16):
        rp = jnp.where(rows16 == r, rp_ref[r], rp)
    decode_pos = jnp.zeros((16, 128), jnp.int32)
    for p in range(PROMPTS):
        decode_pos = jnp.where(rp == p, len_ref[p], decode_pos)
    tables = rope_tables(decode_pos.astype(F32))
    sums = jnp.sum(ss[:, 4:6], axis=0).reshape(16, 128)
    inverse = lax.rsqrt(sums / feature_count + EPS)
    for h in range(4):
        dqg[me_c, :, h * HD : (h + 1) * HD] = head(
            acc_q[:, h * HD : (h + 1) * HD] * inverse, qg, tables
        )
    for h in range(2):
        dk_s[:, h * HD : (h + 1) * HD] = head(
            acc_kv[:, h * HD : (h + 1) * HD] * inverse, kg, tables
        )
        dv_s[:, h * HD : (h + 1) * HD] = (
            acc_kv[:, 256 + h * HD : 256 + (h + 1) * HD] * inverse
        ).astype(BF16)

    def dq1(j, owner_z, target_z):
        slot = dqg.at[ctx_of(y, owner_z)]
        return pltpu.make_async_remote_copy(
            src_ref=slot, dst_ref=slot, send_sem=dq1_send.at[j - 1], recv_sem=dq1_recv.at[j - 1],
            device_id=(ctx_of(y, target_z), me_t), device_id_type=MESH,
        )

    def dq2(j, owner_y, target_y):
        slots = dqg.at[pl.ds(lax.rem(owner_y + NY, NY) * NZ, NZ)]
        return pltpu.make_async_remote_copy(
            src_ref=slots, dst_ref=slots, send_sem=dq2_send.at[j - 1], recv_sem=dq2_recv.at[j - 1],
            device_id=(ctx_of(target_y, z), me_t), device_id_type=MESH,
        )

    for j in range(1, NZ):
        dq1(j, z, z + j).start()

    row_index = lax.broadcasted_iota(jnp.int32, (CH, 1), 0)
    take(1)
    start_own(3)

    def chunk_of(s):
        sums = jnp.sum(jnp.transpose(jnp.sum(ss[:, s], axis=0)), axis=1, keepdims=True)
        inverse = lax.rsqrt(sums / feature_count + EPS)
        tables = rope_tables((block * 512 + s * CH + row_index).astype(F32))
        return xg[s].reshape(8 * feat, CH), inverse, tables

    def project_query(s, states, inverse, tables):
        acc = dot(states, wq[...], ((0,), (0,)))
        for h in range(4):
            q_s[s, :, h * HD : (h + 1) * HD] = head(
                acc[:, h * HD : (h + 1) * HD] * inverse, qg, tables
            )

    def project(s, carry):
        @pl.when((s >= 1) & (s < NCH - 1))
        def _():
            take(s + 1)

        finish(s)
        states, inverse, tables = chunk_of(s)
        acc = dot(states, wkv[...], ((0,), (0,)))
        for h in range(2):
            kv[8 + s, :, h * HD : (h + 1) * HD] = head(
                acc[:, h * HD : (h + 1) * HD] * inverse, kg, tables
            )
        kv[8 + s, :, 256:512] = (acc[:, 256:512] * inverse).astype(BF16)
        halo(0, s).start()
        halo(1, s).start()

        @pl.when(s < NCH - 1)
        def _():
            project_query(s, states, inverse, tables)

        @pl.when(s == 1)
        def _():
            for j in range(1, NZ):
                dq1(j, z - j, z).wait_recv()
            for j in range(1, NY):
                dq2(j, y, y + j).start()

        return carry

    lax.fori_loop(0, NCH, project, 0)

    for j in range(1, NY):
        dq2(j, y - j, y).wait_recv()
    length = len_ref[prompt]
    key_pos = block * 512 + lax.broadcasted_iota(jnp.int32, (1, 512), 1)
    bias = jnp.where((key_pos >= length - WINDOW) & (key_pos < length), 0.0, NEG)
    lane = lax.broadcasted_iota(jnp.int32, (1, 128), 1)

    def pack(columns):
        both = jnp.where(lane < 2, *[jnp.where(lane % 2 == 0, *columns[k : k + 2]) for k in (0, 2)])
        both = jnp.where(lane < 4, both, 0.0)
        high = both.astype(BF16).astype(F32)
        middle = (both - high).astype(BF16).astype(F32)
        low = both - high - middle
        return (high + pltpu.roll(middle, 4, axis=1) + pltpu.roll(low, 8, axis=1)).astype(BF16)

    def unpack(packed):
        wide = packed.astype(F32)
        return wide + pltpu.roll(wide, 124, axis=1) + pltpu.roll(wide, 120, axis=1)

    queries = dqg[...].reshape(512, 512)
    keys = kv[8:12].reshape(512, 512)
    lse_list = []
    for h in range(4):
        g = h // 2
        scores = dot(
            queries[:, h * HD : (h + 1) * HD], keys[:, g * HD : (g + 1) * HD], ((1,), (1,))
        )
        scores = scores * LOG2_SCALE + bias
        top = jnp.max(scores, axis=1, keepdims=True)
        weights_h = jnp.exp2(scores - top)
        total = jnp.sum(weights_h, axis=1, keepdims=True)
        mixed = dot(
            weights_h.astype(BF16), keys[:, 256 + g * HD : 256 + (g + 1) * HD], ((1,), (0,))
        )
        dpart[:, :, h * HD : (h + 1) * HD] = (mixed * (1.0 / total)).astype(BF16).reshape(32, 16, HD)
        lse_list.append(top + jnp.log2(total))
    dpart[:, :, 512:640] = pack(lse_list).reshape(32, 16, 128)

    def r1(j, slot_y, target_y):
        return pltpu.make_async_remote_copy(
            src_ref=dpart.at[pl.ds(lax.rem(target_y + NY, NY) * NZ, NZ)],
            dst_ref=b1.at[lax.rem(slot_y + NY, NY)],
            send_sem=r1_send.at[j - 1], recv_sem=r1_recv.at[j - 1],
            device_id=(ctx_of(target_y, z), me_t), device_id_type=MESH,
        )

    def r2(j, slot_z, target_z):
        return pltpu.make_async_remote_copy(
            src_ref=p2.at[lax.rem(target_z + NZ, NZ)],
            dst_ref=b2.at[lax.rem(slot_z + NZ, NZ)],
            send_sem=r2_send.at[j - 1], recv_sem=r2_recv.at[j - 1],
            device_id=(ctx_of(y, target_z), me_t), device_id_type=MESH,
        )

    for j in range(1, NY):
        r1(j, y, y + j).start()
    b1[y] = dpart[pl.ds(y * NZ, NZ)]
    project_query(NCH - 1, *chunk_of(NCH - 1))

    def query_of(i, g):
        return jnp.concatenate(
            [q_s[i, :, (2 * g + r) * HD : (2 * g + r + 1) * HD] for r in range(2)], axis=0
        )

    def softmax(scores, window, g):
        top = jnp.max(scores, axis=1, keepdims=True) * LOG2_SCALE
        weights_h = jnp.exp2(scores * LOG2_SCALE - top)
        total = jnp.sum(weights_h, axis=1, keepdims=True)
        values = window[:, 256 + g * HD : 256 + (g + 1) * HD]
        return top, total, dot(weights_h.astype(BF16), values, ((1,), (0,)))

    for s in range(NCH):
        halo(0, s).wait_recv()
    width = 5 * CH
    rows2 = lax.rem(lax.broadcasted_iota(jnp.int32, (2 * CH, 1), 0), CH)
    cols = lax.broadcasted_iota(jnp.int32, (1, CH), 1)
    columns = lax.broadcasted_iota(jnp.int32, (1, width), 1)

    def attend_first(i, carry):
        low = jnp.where((block >= 2) | (columns >= (4 - i) * CH), 0.0, NEG)
        for g in range(2):
            window = kv[pl.ds(4 + i, 5)].reshape(width, 512)
            scores = dot(query_of(i, g), window[:, g * HD : (g + 1) * HD], ((1,), (1,)))
            scores = scores + low
            scores = jnp.concatenate(
                [
                    jnp.where(cols > rows2, scores[:, :CH], NEG),
                    scores[:, CH : 4 * CH],
                    jnp.where(cols <= rows2, scores[:, 4 * CH :], NEG),
                ],
                axis=1,
            )
            top, total, mixed = softmax(scores, window, g)
            top_s[i, g], sum_s[i, g], mix_s[i, g] = top, total, mixed
        return carry

    lax.fori_loop(0, NCH, attend_first, 0)
    for j in range(1, NY):
        r1(j, y - j, y).wait_recv()

    def merge(parts, lses):
        top = functools.reduce(jnp.maximum, lses)
        factors = [jnp.exp2(lse - top) for lse in lses]
        total = sum(factors)
        mixed = [
            sum(
                f[:, h : h + 1] * part[:, h * HD : (h + 1) * HD].astype(F32)
                for f, part in zip(factors, parts)
            )
            for h in range(4)
        ]
        return top, total, mixed

    parts = [b1[i].reshape(128, 640) for i in range(NY)]
    top, total, mixed = merge(parts, [unpack(part[:, 512:640]) for part in parts])
    share = 1.0 / total
    for h in range(4):
        p2[:, :, h * HD : (h + 1) * HD] = (
            (mixed[h] * share[:, h : h + 1]).astype(BF16).reshape(8, 16, HD)
        )
    lse = top + jnp.log2(total)
    p2[:, :, 512:640] = pack([lse[:, h : h + 1] for h in range(4)]).reshape(8, 16, 128)
    for j in range(1, NZ):
        r2(j, z, z + j).start()
    b2[z] = p2[z]

    for s in range(NCH):
        halo(1, s).wait_recv()

    def attend_last(i, carry):
        alive = block * 512 + i * CH + rows2 < length
        for g in range(2):
            window = kv[0:4].reshape(512, 512)
            scores = dot(query_of(i, g), window[:, g * HD : (g + 1) * HD], ((1,), (1,)))
            top, total, mixed = softmax(scores, window, g)
            top = jnp.where(block == 0, NEG, top)
            first_top = top_s[i, g]
            both = jnp.maximum(top, first_top)
            f1, f2 = jnp.exp2(first_top - both), jnp.exp2(top - both)
            share = 1.0 / (sum_s[i, g] * f1 + total * f2)
            mixed = mix_s[i, g] * (f1 * share) + mixed * (f2 * share)
            mixed = jnp.where(alive, mixed, 0.0).astype(BF16)
            for r in range(2):
                out_ref[
                    pl.ds(pl.multiple_of(i * CH, CH), CH),
                    (2 * g + r) * HD : (2 * g + r + 1) * HD,
                ] = mixed[r * CH : (r + 1) * CH]
        return carry

    lax.fori_loop(0, NCH, attend_last, 0)

    for j in range(1, NZ):
        r2(j, z - j, z).wait_recv()
    parts = [b2[i] for i in range(NZ)]
    lses = [
        jnp.where(rp == i % PROMPTS, unpack(part[:, 512:640]), NEG) for i, part in enumerate(parts)
    ]
    tops, totals, mixed = merge(parts, lses)
    own_query = dqg[me_c].astype(F32)
    for h in range(4):
        g = h // 2
        top, total = tops[:, h : h + 1], totals[:, h : h + 1]
        own = (
            jnp.sum(
                own_query[:, h * HD : (h + 1) * HD]
                * dk_s[:, g * HD : (g + 1) * HD].astype(F32),
                axis=1,
                keepdims=True,
            )
            * LOG2_SCALE
        )
        new_top = jnp.maximum(top, own)
        shift = jnp.exp2(top - new_top)
        weight = jnp.exp2(own - new_top)
        value = dv_s[:, g * HD : (g + 1) * HD].astype(F32)
        dout_ref[:, h * HD : (h + 1) * HD] = (
            (mixed[h] * shift + weight * value) / (total * shift + weight)
        ).astype(BF16)

    for k in range(6):
        ag_sent(k)
    for s in range(NCH):
        for kind in range(2):
            halo(kind, s).wait_send()
    for j in range(1, NZ):
        dq1(j, z, z + j).wait_send()
        r2(j, z, z + j).wait_send()
    for j in range(1, NY):
        dq2(j, y, y + j).wait_send()
        r1(j, y, y + j).wait_send()


def hand_over(a_ref, b_ref, a_out, b_out):
    a_out[...] = a_ref[...]
    b_out[...] = b_ref[...]


def local(
    prompt_states,
    decode_states,
    norm_gain,
    query_weight,
    key_weight,
    value_weight,
    query_gain,
    key_gain,
    prompt_lengths,
    row_prompt,
):
    tok_rows, feat = prompt_states.shape
    dec_rows = decode_states.shape[0]
    feature_count = norm_gain.shape[0]
    half = HD // 2
    frequency = np.array([10000.0 ** (-2.0 * (j % half) / HD) for j in range(HD)], np.float32)
    sign = np.array([-1.0] * half + [1.0] * half, np.float32)
    vmem = pl.BlockSpec(memory_space=pltpu.VMEM)
    hbm = pl.BlockSpec(memory_space=pl.ANY)
    dma = pltpu.SemaphoreType.DMA
    attended = pl.pallas_call(
        functools.partial(kernel, float(feature_count)),
        out_shape=(
            jax.ShapeDtypeStruct((tok_rows, 512), BF16),
            jax.ShapeDtypeStruct((dec_rows, 512), BF16),
        ),
        in_specs=[vmem] * 7 + [pl.BlockSpec(memory_space=pltpu.SMEM)] * 2 + [hbm] * 3,
        out_specs=(vmem, vmem),
        scratch_shapes=[
            pltpu.VMEM((NCH, 8, feat, CH), BF16),
            pltpu.VMEM((8, dec_rows, feat), BF16),
            pltpu.VMEM((8, 6, 8, 128), F32),
            pltpu.VMEM((feature_count, 512), BF16),
            pltpu.VMEM((feature_count, 512), BF16),
            pltpu.VMEM((12, CH, 512), BF16),
            pltpu.VMEM((NCH, CH, 512), BF16),
            pltpu.VMEM((32, dec_rows, 512), BF16),
            pltpu.VMEM((dec_rows, 256), BF16),
            pltpu.VMEM((dec_rows, 256), BF16),
            pltpu.VMEM((32, dec_rows, 640), BF16),
            pltpu.VMEM((NY, NZ, dec_rows, 640), BF16),
            pltpu.VMEM((NZ, dec_rows, 640), BF16),
            pltpu.VMEM((NZ, dec_rows, 640), BF16),
            pltpu.VMEM((NCH, 2, 2 * CH, 1), F32),
            pltpu.VMEM((NCH, 2, 2 * CH, 1), F32),
            pltpu.VMEM((NCH, 2, 2 * CH, HD), F32),
            pltpu.VMEM((feature_count, 128), F32),
            dma((6, 7)), dma((6, 7)), dma((3,)), dma((2, NCH)), dma((2, NCH)),
            dma((NZ - 1,)), dma((NZ - 1,)), dma((NY - 1,)), dma((NY - 1,)),
            dma((NY - 1,)), dma((NY - 1,)), dma((NZ - 1,)), dma((NZ - 1,)),
        ],
        compiler_params=pltpu.CompilerParams(
            collective_id=0, has_side_effects=True, vmem_limit_bytes=60 * 2**20
        ),
    )(
        prompt_states.T,
        decode_states,
        norm_gain.reshape(-1, 128),
        jnp.asarray(frequency)[None, :],
        jnp.asarray(sign)[None, :],
        query_gain[None, :],
        key_gain[None, :],
        prompt_lengths,
        row_prompt,
        query_weight,
        key_weight,
        value_weight,
    )
    return pl.pallas_call(
        hand_over,
        out_shape=tuple(jax.ShapeDtypeStruct(a.shape, a.dtype) for a in attended),
        in_specs=[vmem] * 2,
        out_specs=(vmem, vmem),
    )(*attended)


def solution(mesh):
    placed = (
        P("ctx", "tp"),
        P("ctx", "tp"),
        P(),
        P(None, "tp"),
        P(None, "tp"),
        P(None, "tp"),
        P(),
        P(),
        P(),
        P("ctx"),
    )
    return jax.shard_map(
        local,
        mesh=mesh,
        in_specs=placed,
        out_specs=(P("ctx", "tp"), P("ctx", "tp")),
        check_vma=False,
    )
```

```python
import functools
import math

import jax
import jax.numpy as jnp
import numpy as np
from jax import lax
from jax.experimental import pallas as pl
from jax.experimental.pallas import tpu as pltpu
from jax.sharding import PartitionSpec as P

MESH = pl.DeviceIdType.MESH
F32, BF16 = jnp.float32, jnp.bfloat16
WINDOW = 1024
PROMPTS = 4
EPS = 1e-06
SCORE_SCALE = 168.0 ** (-0.5)
LOG2_SCALE = SCORE_SCALE * math.log2(math.e)
HD = 128
NY, NZ, NX = 4, 8, 4
CH = 128
NCH = 4
NEG = -1e30


def dot(a, b, dims):
    return lax.dot_general(a, b, (dims, ((), ())), preferred_element_type=F32)


def kernel(
    feature_count,
    x_ref, xd_ref, gain_ref, freq_ref, sgn_ref, qg_ref, kg_ref, len_ref, rp_ref,
    wq_hbm, wk_hbm, wv_hbm,
    out_ref, dout_ref,
    xg, xd, ss, wkv, wq, kv, q_s, dqg, dk_s, dv_s, dpart, b1, p2, b2, top_s, sum_s, mix_s, gain_s,
    ag_send, ag_recv, wsem, h_send, h_recv,
    dq1_send, dq1_recv, dq2_send, dq2_recv, r1_send, r1_recv, r2_send, r2_recv,
):
    me_c = lax.axis_index("ctx")
    me_t = lax.axis_index("tp")
    x, c = me_t // 2, lax.rem(me_t, 2)
    y, z = me_c // NZ, lax.rem(me_c, NZ)
    way = 1 - 2 * c
    feat = x_ref.shape[0]
    block = 2 * y + z // 4
    prompt = lax.rem(z, PROMPTS)

    def tp_of(xx, cc):
        return lax.rem(xx + NX, NX) * 2 + cc

    def ctx_of(yy, zz):
        return lax.rem(yy + NY, NY) * NZ + lax.rem(zz + NZ, NZ)

    near_a, near_b, far = tp_of(x - way, c), tp_of(x + way, c), tp_of(x + 2, c)
    partner = tp_of(x, 1 - c)
    from_partner = (partner, tp_of(x + way, 1 - c), tp_of(x - way, 1 - c), tp_of(x + 2, 1 - c))
    out_b1 = ctx_of(y + z // 4, z + 4)
    in_b1 = ctx_of(y - (1 - z // 4), z + 4)

    weights = (
        pltpu.make_async_copy(wk_hbm, wkv.at[:, 0:256], wsem.at[0]),
        pltpu.make_async_copy(wv_hbm, wkv.at[:, 256:512], wsem.at[1]),
        pltpu.make_async_copy(wq_hbm, wq, wsem.at[2]),
    )
    for copy in weights:
        copy.start()

    barrier = pltpu.get_barrier_semaphore()
    for device in (
        [(me_c, t) for t in (near_a, near_b, partner)]
        + [(ctx_of(y, z + j), me_t) for j in range(1, NZ)]
        + [(ctx_of(y + j, z), me_t) for j in range(1, NY)]
        + [(in_b1, me_t)]
    ):
        pl.semaphore_signal(barrier, inc=1, device_id=device, device_id_type=MESH)

    gains = gain_ref.shape[0]
    padded = jnp.concatenate([gain_ref[...], jnp.zeros((128 - gains, 128), F32)], axis=0)
    columns_of = jnp.transpose(padded)
    for r in range(gains):
        gain_s[r * 128 : (r + 1) * 128] = jnp.broadcast_to(columns_of[:, r : r + 1], (128, 128))
    gain_column = gain_s[pl.ds(pl.multiple_of(me_t * feat, 32), feat), :]
    gain_row = jnp.transpose(
        jnp.concatenate([gain_column, jnp.zeros((-feat % 128, 128), F32)], axis=0)
    )[0:1, :feat]
    decode_wide = xd_ref[...].astype(F32)
    xd[me_t] = (decode_wide * gain_row).astype(BF16)
    decode_sum = jnp.sum(decode_wide * decode_wide, axis=1, keepdims=True)
    ss[me_t, 4:6] = jnp.broadcast_to(decode_sum, (16, 128)).reshape(2, 8, 128)
    for k in range(NCH):
        wide = x_ref[:, k * CH : (k + 1) * CH].astype(F32)
        xg[k, me_t] = (wide * gain_column).astype(BF16).reshape(2, feat // 2, CH)
        ss[me_t, k] = jnp.sum((wide * wide).reshape(feat // 8, 8, CH), axis=0)

    pl.semaphore_wait(barrier, 14)

    def piece(k, d):
        if isinstance(k, int) and k == 8:
            return xd.at[d]
        if isinstance(k, int) and k == 9:
            return ss.at[d]
        return xg.at[lax.div(k, 2), d, lax.rem(k, 2)]

    def ag(k, d, j, target):
        return pltpu.make_async_remote_copy(
            src_ref=piece(k, d), dst_ref=piece(k, d),
            send_sem=ag_send.at[k, j], recv_sem=ag_recv.at[k, j],
            device_id=(me_c, target), device_id_type=MESH,
        )

    def start_own(k):
        ag(k, me_t, 0, near_b).start()
        ag(k, me_t, 1, near_a).start()
        ag(k, me_t, 3, partner).start()

    def take(k):
        ag(k, near_a, 0, near_b).wait_recv()
        ag(k, near_a, 2, near_b).start()
        ag(k, near_a, 4, partner).start()
        ag(k, near_b, 1, near_b).wait_recv()
        ag(k, near_b, 5, partner).start()

    def finish(k):
        ag(k, far, 2, near_b).wait_recv()
        ag(k, far, 6, partner).start()
        for j in range(4):
            ag(k, from_partner[j], 3 + j, near_b).wait_recv()

    def ag_sent(k):
        for j in range(7):
            ag(k, me_t, j, near_b).wait_send()

    def halo(kind, s):
        slot, target = ((4 + s, ctx_of(y + 1, z)), (s, out_b1))[kind]
        return pltpu.make_async_remote_copy(
            src_ref=kv.at[8 + s], dst_ref=kv.at[slot],
            send_sem=h_send.at[kind, s], recv_sem=h_recv.at[kind, s],
            device_id=(target, me_t), device_id_type=MESH,
        )

    freq, sgn = freq_ref[...], sgn_ref[...]

    def rope_tables(positions):
        angles = positions * freq
        return jnp.cos(angles), jnp.sin(angles) * sgn

    def head(acc, gain, tables):
        unit = acc * lax.rsqrt(jnp.mean(acc * acc, axis=1, keepdims=True) + EPS) * gain
        return (unit * tables[0] + pltpu.roll(unit, HD // 2, axis=1) * tables[1]).astype(BF16)

    qg, kg = qg_ref[...], kg_ref[...]

    for k in (9, 8, 0, 1):
        start_own(k)
    for k in (9, 8, 0, 1):
        take(k)
    for k in (2, 3):
        start_own(k)
    for k in (9, 8):
        finish(k)

    rows16 = lax.broadcasted_iota(jnp.int32, (16, 128), 0)
    rp = jnp.zeros((16, 128), jnp.int32)
    for r in range(16):
        rp = jnp.where(rows16 == r, rp_ref[r], rp)
    decode_pos = jnp.zeros((16, 128), jnp.int32)
    for p in range(PROMPTS):
        decode_pos = jnp.where(rp == p, len_ref[p], decode_pos)
    def dq1(j, owner_z, target_z):
        slot = dqg.at[ctx_of(y, owner_z)]
        return pltpu.make_async_remote_copy(
            src_ref=slot, dst_ref=slot, send_sem=dq1_send.at[j - 1], recv_sem=dq1_recv.at[j - 1],
            device_id=(ctx_of(y, target_z), me_t), device_id_type=MESH,
        )

    def dq2(j, owner_y, target_y):
        slots = dqg.at[pl.ds(lax.rem(owner_y + NY, NY) * NZ, NZ)]
        return pltpu.make_async_remote_copy(
            src_ref=slots, dst_ref=slots, send_sem=dq2_send.at[j - 1], recv_sem=dq2_recv.at[j - 1],
            device_id=(ctx_of(target_y, z), me_t), device_id_type=MESH,
        )


    def project_decode():
        acc_kv = jnp.zeros((16, 512), F32)
        acc_q = jnp.zeros((16, 512), F32)
        for d in range(8):
            rows = slice(d * feat, (d + 1) * feat)
            acc_kv += dot(xd[d], wkv[rows, :], ((1,), (0,)))
            acc_q += dot(xd[d], wq[rows, :], ((1,), (0,)))
        tables = rope_tables(decode_pos.astype(F32))
        sums = jnp.sum(ss[:, 4:6], axis=0).reshape(16, 128)
        inverse = lax.rsqrt(sums / feature_count + EPS)
        for h in range(4):
            dqg[me_c, :, h * HD : (h + 1) * HD] = head(
                acc_q[:, h * HD : (h + 1) * HD] * inverse, qg, tables
            )
        for h in range(2):
            dk_s[:, h * HD : (h + 1) * HD] = head(
                acc_kv[:, h * HD : (h + 1) * HD] * inverse, kg, tables
            )
            dv_s[:, h * HD : (h + 1) * HD] = (
                acc_kv[:, 256 + h * HD : 256 + (h + 1) * HD] * inverse
            ).astype(BF16)

        for j in range(1, NZ):
            dq1(j, z, z + j).start()

    row_index = lax.broadcasted_iota(jnp.int32, (CH, 1), 0)
    weights[0].wait()
    weights[1].wait()

    def chunk_of(s):
        sums = jnp.sum(jnp.transpose(jnp.sum(ss[:, s], axis=0)), axis=1, keepdims=True)
        inverse = lax.rsqrt(sums / feature_count + EPS)
        tables = rope_tables((block * 512 + s * CH + row_index).astype(F32))
        return xg[s].reshape(8 * feat, CH), inverse, tables

    def project_query(s, states, inverse, tables):
        acc = dot(states, wq[...], ((0,), (0,)))
        for h in range(4):
            q_s[s, :, h * HD : (h + 1) * HD] = head(
                acc[:, h * HD : (h + 1) * HD] * inverse, qg, tables
            )

    def project(s, carry):
        finish(2 * s)
        finish(2 * s + 1)
        states, inverse, tables = chunk_of(s)
        acc = dot(states, wkv[...], ((0,), (0,)))
        for h in range(2):
            kv[8 + s, :, h * HD : (h + 1) * HD] = head(
                acc[:, h * HD : (h + 1) * HD] * inverse, kg, tables
            )
        kv[8 + s, :, 256:512] = (acc[:, 256:512] * inverse).astype(BF16)
        halo(0, s).start()
        halo(1, s).start()

        @pl.when(s < NCH - 1)
        def _():
            take(2 * s + 2)
            take(2 * s + 3)

        @pl.when(s < NCH - 2)
        def _():
            start_own(2 * s + 4)
            start_own(2 * s + 5)

        @pl.when(s == 0)
        def _():
            weights[2].wait()
            project_decode()

        @pl.when(s < NCH - 1)
        def _():
            project_query(s, states, inverse, tables)

        @pl.when(s == 1)
        def _():
            for j in range(1, NZ):
                dq1(j, z - j, z).wait_recv()
            for j in range(1, NY):
                dq2(j, y, y + j).start()

        return carry

    lax.fori_loop(0, NCH, project, 0)

    for j in range(1, NY):
        dq2(j, y - j, y).wait_recv()
    length = len_ref[prompt]
    key_pos = block * 512 + lax.broadcasted_iota(jnp.int32, (1, 512), 1)
    bias = jnp.where((key_pos >= length - WINDOW) & (key_pos < length), 0.0, NEG)
    lane = lax.broadcasted_iota(jnp.int32, (1, 128), 1)

    def pack(columns):
        both = jnp.where(lane < 2, *[jnp.where(lane % 2 == 0, *columns[k : k + 2]) for k in (0, 2)])
        both = jnp.where(lane < 4, both, 0.0)
        high = both.astype(BF16).astype(F32)
        middle = (both - high).astype(BF16).astype(F32)
        low = both - high - middle
        return (high + pltpu.roll(middle, 4, axis=1) + pltpu.roll(low, 8, axis=1)).astype(BF16)

    def unpack(packed):
        wide = packed.astype(F32)
        return wide + pltpu.roll(wide, 124, axis=1) + pltpu.roll(wide, 120, axis=1)

    def r1(j, slot_y, target_y):
        return pltpu.make_async_remote_copy(
            src_ref=dpart.at[pl.ds(lax.rem(target_y + NY, NY) * NZ, NZ)],
            dst_ref=b1.at[lax.rem(slot_y + NY, NY)],
            send_sem=r1_send.at[j - 1], recv_sem=r1_recv.at[j - 1],
            device_id=(ctx_of(target_y, z), me_t), device_id_type=MESH,
        )

    def send_parts():
        for j in range(1, NY):
            r1(j, y, y + j).start()

    queries = dqg[...].reshape(512, 512)
    keys = kv[8:12].reshape(512, 512)
    lse_list = []
    for h in range(4):
        g = h // 2
        scores = dot(
            queries[:, h * HD : (h + 1) * HD], keys[:, g * HD : (g + 1) * HD], ((1,), (1,))
        )
        scores = scores * LOG2_SCALE + bias
        top = jnp.max(scores, axis=1, keepdims=True)
        weights_h = jnp.exp2(scores - top)
        total = jnp.sum(weights_h, axis=1, keepdims=True)
        mixed = dot(
            weights_h.astype(BF16), keys[:, 256 + g * HD : 256 + (g + 1) * HD], ((1,), (0,))
        )
        dpart[:, :, h * HD : (h + 1) * HD] = (mixed * (1.0 / total)).astype(BF16).reshape(32, 16, HD)
        lse_list.append(top + jnp.log2(total))
    dpart[:, :, 512:640] = pack(lse_list).reshape(32, 16, 128)
    send_parts()

    def r2(j, slot_z, target_z):
        return pltpu.make_async_remote_copy(
            src_ref=p2.at[lax.rem(target_z + NZ, NZ)],
            dst_ref=b2.at[lax.rem(slot_z + NZ, NZ)],
            send_sem=r2_send.at[j - 1], recv_sem=r2_recv.at[j - 1],
            device_id=(ctx_of(y, target_z), me_t), device_id_type=MESH,
        )

    b1[y] = dpart[pl.ds(y * NZ, NZ)]
    project_query(NCH - 1, *chunk_of(NCH - 1))

    def query_of(i, g):
        return jnp.concatenate(
            [q_s[i, :, (2 * g + r) * HD : (2 * g + r + 1) * HD] for r in range(2)], axis=0
        )

    def softmax(scores, window, g):
        top = jnp.max(scores, axis=1, keepdims=True) * LOG2_SCALE
        weights_h = jnp.exp2(scores * LOG2_SCALE - top)
        total = jnp.sum(weights_h, axis=1, keepdims=True)
        values = window[:, 256 + g * HD : 256 + (g + 1) * HD]
        return top, total, dot(weights_h.astype(BF16), values, ((1,), (0,)))

    for s in range(NCH):
        halo(0, s).wait_recv()
    width = 5 * CH
    rows2 = lax.rem(lax.broadcasted_iota(jnp.int32, (2 * CH, 1), 0), CH)
    cols = lax.broadcasted_iota(jnp.int32, (1, CH), 1)
    columns = lax.broadcasted_iota(jnp.int32, (1, width), 1)

    def attend_first(i, carry):
        low = jnp.where((block >= 2) | (columns >= (4 - i) * CH), 0.0, NEG)
        for g in range(2):
            window = kv[pl.ds(4 + i, 5)].reshape(width, 512)
            scores = dot(query_of(i, g), window[:, g * HD : (g + 1) * HD], ((1,), (1,)))
            scores = scores + low
            scores = jnp.concatenate(
                [
                    jnp.where(cols > rows2, scores[:, :CH], NEG),
                    scores[:, CH : 4 * CH],
                    jnp.where(cols <= rows2, scores[:, 4 * CH :], NEG),
                ],
                axis=1,
            )
            top, total, mixed = softmax(scores, window, g)
            top_s[i, g], sum_s[i, g], mix_s[i, g] = top, total, mixed
        return carry

    lax.fori_loop(0, NCH, attend_first, 0)
    for j in range(1, NY):
        r1(j, y - j, y).wait_recv()

    def merge(part_of, count, lses):
        top = functools.reduce(jnp.maximum, lses)
        factors = [jnp.exp2(lse - top) for lse in lses]
        total = sum(factors)
        mixed = [
            sum(
                factors[i][:, h : h + 1] * part_of(i, h).astype(F32) for i in range(count)
            )
            for h in range(4)
        ]
        return top, total, mixed

    def over_y(i, h):
        return b1[i, :, :, h * HD : (h + 1) * HD].reshape(128, HD)

    top, total, mixed = merge(over_y, NY, [unpack(over_y(i, 4)) for i in range(NY)])
    share = 1.0 / total
    for h in range(4):
        p2[:, :, h * HD : (h + 1) * HD] = (
            (mixed[h] * share[:, h : h + 1]).astype(BF16).reshape(8, 16, HD)
        )
    lse = top + jnp.log2(total)
    p2[:, :, 512:640] = pack([lse[:, h : h + 1] for h in range(4)]).reshape(8, 16, 128)
    for j in range(1, NZ):
        r2(j, z, z + j).start()
    b2[z] = p2[z]

    for s in range(NCH):
        halo(1, s).wait_recv()

    def attend_last(i, carry):
        alive = block * 512 + i * CH + rows2 < length
        for g in range(2):
            window = kv[0:4].reshape(512, 512)
            scores = dot(query_of(i, g), window[:, g * HD : (g + 1) * HD], ((1,), (1,)))
            top, total, mixed = softmax(scores, window, g)
            top = jnp.where(block == 0, NEG, top)
            first_top = top_s[i, g]
            both = jnp.maximum(top, first_top)
            f1, f2 = jnp.exp2(first_top - both), jnp.exp2(top - both)
            share = 1.0 / (sum_s[i, g] * f1 + total * f2)
            mixed = mix_s[i, g] * (f1 * share) + mixed * (f2 * share)
            mixed = jnp.where(alive, mixed, 0.0).astype(BF16)
            for r in range(2):
                out_ref[
                    pl.ds(pl.multiple_of(i * CH, CH), CH),
                    (2 * g + r) * HD : (2 * g + r + 1) * HD,
                ] = mixed[r * CH : (r + 1) * CH]
        return carry

    lax.fori_loop(0, NCH, attend_last, 0)

    for j in range(1, NZ):
        r2(j, z - j, z).wait_recv()
    def over_z(i, h):
        return b2[i, :, h * HD : (h + 1) * HD]

    lses = [jnp.where(rp == i % PROMPTS, unpack(over_z(i, 4)), NEG) for i in range(NZ)]
    tops, totals, mixed = merge(over_z, NZ, lses)
    own_query = dqg[me_c].astype(F32)
    for h in range(4):
        g = h // 2
        top, total = tops[:, h : h + 1], totals[:, h : h + 1]
        own = (
            jnp.sum(
                own_query[:, h * HD : (h + 1) * HD]
                * dk_s[:, g * HD : (g + 1) * HD].astype(F32),
                axis=1,
                keepdims=True,
            )
            * LOG2_SCALE
        )
        new_top = jnp.maximum(top, own)
        shift = jnp.exp2(top - new_top)
        weight = jnp.exp2(own - new_top)
        value = dv_s[:, g * HD : (g + 1) * HD].astype(F32)
        dout_ref[:, h * HD : (h + 1) * HD] = (
            (mixed[h] * shift + weight * value) / (total * shift + weight)
        ).astype(BF16)

    for k in range(10):
        ag_sent(k)
    for s in range(NCH):
        for kind in range(2):
            halo(kind, s).wait_send()
    for j in range(1, NZ):
        dq1(j, z, z + j).wait_send()
        r2(j, z, z + j).wait_send()
    for j in range(1, NY):
        dq2(j, y, y + j).wait_send()
        r1(j, y, y + j).wait_send()


def hand_over(a_ref, b_ref, a_out, b_out):
    a_out[...] = a_ref[...]
    b_out[...] = b_ref[...]


def local(
    prompt_states,
    decode_states,
    norm_gain,
    query_weight,
    key_weight,
    value_weight,
    query_gain,
    key_gain,
    prompt_lengths,
    row_prompt,
):
    tok_rows, feat = prompt_states.shape
    dec_rows = decode_states.shape[0]
    feature_count = norm_gain.shape[0]
    half = HD // 2
    frequency = np.array([10000.0 ** (-2.0 * (j % half) / HD) for j in range(HD)], np.float32)
    sign = np.array([-1.0] * half + [1.0] * half, np.float32)
    vmem = pl.BlockSpec(memory_space=pltpu.VMEM)
    hbm = pl.BlockSpec(memory_space=pl.ANY)
    dma = pltpu.SemaphoreType.DMA
    attended = pl.pallas_call(
        functools.partial(kernel, float(feature_count)),
        out_shape=(
            jax.ShapeDtypeStruct((tok_rows, 512), BF16),
            jax.ShapeDtypeStruct((dec_rows, 512), BF16),
        ),
        in_specs=[vmem] * 7 + [pl.BlockSpec(memory_space=pltpu.SMEM)] * 2 + [hbm] * 3,
        out_specs=(vmem, vmem),
        scratch_shapes=[
            pltpu.VMEM((NCH, 8, 2, feat // 2, CH), BF16),
            pltpu.VMEM((8, dec_rows, feat), BF16),
            pltpu.VMEM((8, 6, 8, 128), F32),
            pltpu.VMEM((feature_count, 512), BF16),
            pltpu.VMEM((feature_count, 512), BF16),
            pltpu.VMEM((12, CH, 512), BF16),
            pltpu.VMEM((NCH, CH, 512), BF16),
            pltpu.VMEM((32, dec_rows, 512), BF16),
            pltpu.VMEM((dec_rows, 256), BF16),
            pltpu.VMEM((dec_rows, 256), BF16),
            pltpu.VMEM((32, dec_rows, 640), BF16),
            pltpu.VMEM((NY, NZ, dec_rows, 640), BF16),
            pltpu.VMEM((NZ, dec_rows, 640), BF16),
            pltpu.VMEM((NZ, dec_rows, 640), BF16),
            pltpu.VMEM((NCH, 2, 2 * CH, 1), F32),
            pltpu.VMEM((NCH, 2, 2 * CH, 1), F32),
            pltpu.VMEM((NCH, 2, 2 * CH, HD), F32),
            pltpu.VMEM((feature_count, 128), F32),
            dma((10, 7)), dma((10, 7)), dma((3,)), dma((2, NCH)), dma((2, NCH)),
            dma((NZ - 1,)), dma((NZ - 1,)), dma((NY - 1,)), dma((NY - 1,)),
            dma((NY - 1,)), dma((NY - 1,)), dma((NZ - 1,)), dma((NZ - 1,)),
        ],
        compiler_params=pltpu.CompilerParams(
            collective_id=0, has_side_effects=True, vmem_limit_bytes=60 * 2**20
        ),
    )(
        prompt_states.T,
        decode_states,
        norm_gain.reshape(-1, 128),
        jnp.asarray(frequency)[None, :],
        jnp.asarray(sign)[None, :],
        query_gain[None, :],
        key_gain[None, :],
        prompt_lengths,
        row_prompt,
        query_weight,
        key_weight,
        value_weight,
    )
    return pl.pallas_call(
        hand_over,
        out_shape=tuple(jax.ShapeDtypeStruct(a.shape, a.dtype) for a in attended),
        in_specs=[vmem] * 2,
        out_specs=(vmem, vmem),
    )(*attended)


def solution(mesh):
    placed = (
        P("ctx", "tp"),
        P("ctx", "tp"),
        P(),
        P(None, "tp"),
        P(None, "tp"),
        P(None, "tp"),
        P(),
        P(),
        P(),
        P("ctx"),
    )
    return jax.shard_map(
        local,
        mesh=mesh,
        in_specs=placed,
        out_specs=(P("ctx", "tp"), P("ctx", "tp")),
        check_vma=False,
    )
```
